1024 devices in a mesh: seq: 64 (over z, core), head: 16 (over x, y).
Axes of the slice: x: 4, y: 4, z: 32, core: 2. Of those that a mesh axis runs over, the one named last changes fastest.
Arguments:
- queries: bfloat16 [16384, 8192], P('seq', 'head'), may hold values from -6 to 6
- key_states: bfloat16 [16384, 1024], P('seq', 'head'), may hold values from -6 to 6
- value_states: bfloat16 [16384, 1024], P('seq', 'head'), may hold values from -6 to 6
- block_picks: int32 [32, 8, 2], replicated, may hold values from 1 to 31, as said below
- grad_output: bfloat16 [16384, 8192], P('seq', 'head'), may hold values from -6 to 6
Outputs:
- attn_output: bfloat16 [16384, 8192], P('seq', 'head')
- grad_queries: float32 [16384, 8192], P('seq', 'head')
- grad_keys: float32 [16384, 1024], P('seq', 'head')
- grad_values: float32 [16384, 1024], P('seq', 'head')
The draws below stay inside these ranges and needn't reach their ends.
Inputs may be any that keep to these rules, and one draw needn't show every extreme that they name: `block_picks`: for query block b and KV head g the offsets differ from each other and lie in 1 to max(b, 2).
All inputs are finite; a program needn't handle non-finite values.
Results may differ from the reference program's by a relative error of at most 0.0095.
Values may be sent and summed in bfloat16 or wider, within the bound.
No kernel may reach another device: no remote copies, remote signals or barrier semaphores. Data moves between devices by JAX's collectives and lax.ppermute only.
A program may use at most 32 MiB of HBM per device.

```python
import jax
import jax.numpy as jnp
from jax import lax

HEAD_DIM = 128
BLOCK = 512
QH = 64
KVH = 8
SEQ = 16384
NBLK = 32


def draw_queries(key, part):
    draws_base = jnp.clip(jax.random.normal(jax.random.fold_in(key, 1), (SEQ, QH, HEAD_DIM), jnp.float32), -6.0, 6.0)
    return draws_base.reshape(SEQ, QH * HEAD_DIM).astype(jnp.bfloat16)


def draw_key_states(key, part):
    draws_base = jnp.clip(jax.random.normal(jax.random.fold_in(key, 2), (SEQ, KVH, HEAD_DIM), jnp.float32), -6.0, 6.0)
    return draws_base.reshape(SEQ, KVH * HEAD_DIM).astype(jnp.bfloat16)


def draw_block_picks(key, part):
    block_index = jnp.arange(NBLK, dtype=jnp.int32)[:, None]
    reach_max = jnp.maximum(block_index, 2)
    first_pick = jax.random.randint(jax.random.fold_in(key, 3), (NBLK, KVH), 0, 1 << 20, jnp.int32) % reach_max
    last_row = (block_index == NBLK - 1) & (jnp.arange(KVH, dtype=jnp.int32)[None, :] == 0)
    first_pick = jnp.where(last_row, reach_max - 1, first_pick)
    second = jax.random.randint(jax.random.fold_in(key, 4), (NBLK, KVH), 0, 1 << 20, jnp.int32) % (reach_max - 1)
    offset_one = 1 + first_pick
    offset_two = 1 + (first_pick + 1 + second) % reach_max
    return jnp.stack([offset_one, offset_two], -1).astype(jnp.int32)


def steps_of(key, dims, cuts, smallest, top_value):
    gain = 1.0
    for dim, parts in cuts:
        heights = jax.random.uniform(jax.random.fold_in(jax.random.fold_in(key, 6), dim), (parts,), jnp.float32, smallest / len(cuts), top_value / len(cuts))
        gain = gain * jnp.repeat(jnp.exp(heights), dims[dim] // parts).reshape((-1,) + (1,) * (len(dims) - 1 - dim))
    return gain


def normal_values(rng, dims, spread, reach, cuts=(), held_as=jnp.bfloat16):
    entries = spread * jax.random.normal(rng, dims, jnp.float32)
    if cuts:
        entries = entries * steps_of(rng, dims, cuts, -0.22, 0.18)
    return jnp.clip(entries, -reach, reach).astype(held_as)


def setup_inputs(seed: int = 0) -> dict:
    splits = jax.random.split(jax.random.key(seed), 6)
    return {
        "queries": draw_queries(jax.random.fold_in(splits[5], 71), 0),
        "key_states": draw_key_states(jax.random.fold_in(splits[5], 71), 0),
        "value_states": normal_values(splits[2], (SEQ, KVH * HEAD_DIM), 1.0, 6.0, ((0, 64), (1, 16))),
        "block_picks": draw_block_picks(jax.random.fold_in(splits[5], 71), 0),
        "grad_output": normal_values(splits[4], (SEQ, QH * HEAD_DIM), 1.0, 6.0, ((0, 64), (1, 16))),
    }


NEGATIVE = -1.0e30


def reference(queries, key_states, value_states, block_picks, grad_output):
    seq_len = queries.shape[0]
    num_blocks = seq_len // BLOCK
    kv_heads = key_states.shape[1] // HEAD_DIM
    group_size = queries.shape[1] // key_states.shape[1]
    chosen = block_picks.shape[2] + 1
    scaling = HEAD_DIM ** -0.5
    query_cube = queries.reshape(num_blocks, BLOCK, kv_heads, group_size, HEAD_DIM)
    grad_cube = grad_output.reshape(num_blocks, BLOCK, kv_heads, group_size, HEAD_DIM)
    key_cube = key_states.reshape(num_blocks, BLOCK, kv_heads, HEAD_DIM)
    value_cube = value_states.reshape(num_blocks, BLOCK, kv_heads, HEAD_DIM)
    key_count = chosen * BLOCK
    positions = jnp.arange(BLOCK, dtype=jnp.int32)
    slot_index = jnp.arange(key_count, dtype=jnp.int32) // BLOCK
    key_place = jnp.arange(key_count, dtype=jnp.int32) % BLOCK

    def advance(totals, item_index):
        grad_key_acc, grad_value_acc = totals
        block_index = (item_index // kv_heads).astype(jnp.int32)
        head_index = (item_index % kv_heads).astype(jnp.int32)
        zero = jnp.zeros((), jnp.int32)
        q_rows = lax.dynamic_slice(query_cube, (block_index, zero, head_index, zero, zero), (1, BLOCK, 1, group_size, HEAD_DIM))
        q_rows = q_rows.reshape(BLOCK, group_size, HEAD_DIM).astype(jnp.float32)
        g_rows = lax.dynamic_slice(grad_cube, (block_index, zero, head_index, zero, zero), (1, BLOCK, 1, group_size, HEAD_DIM))
        g_rows = g_rows.reshape(BLOCK, group_size, HEAD_DIM).astype(jnp.float32)
        offsets = lax.dynamic_slice(block_picks, (block_index, head_index, zero), (1, 1, chosen - 1)).reshape(chosen - 1)
        selected = jnp.concatenate([block_index[None], block_index - offsets.astype(jnp.int32)])
        usable = selected >= 0
        block_ids = jnp.maximum(selected, 0).astype(jnp.int32)
        head_keys = lax.dynamic_index_in_dim(key_cube, head_index, 2, keepdims=False)
        head_values = lax.dynamic_index_in_dim(value_cube, head_index, 2, keepdims=False)
        key_tile = jnp.take(head_keys, block_ids, axis=0).reshape(key_count, HEAD_DIM).astype(jnp.float32)
        value_tile = jnp.take(head_values, block_ids, axis=0).reshape(key_count, HEAD_DIM).astype(jnp.float32)
        scores = jnp.einsum("rhd,kd->hrk", q_rows, key_tile) * scaling
        allowed = usable[slot_index][None, :] & ((slot_index[None, :] > 0) | (key_place[None, :] <= positions[:, None]))
        scores = jnp.where(allowed[None], scores, NEGATIVE)
        row_max = jnp.max(scores, axis=-1, keepdims=True)
        weights = jnp.exp(scores - row_max)
        probs = weights / jnp.sum(weights, axis=-1, keepdims=True)
        probs_low = lax.optimization_barrier(probs.astype(jnp.bfloat16)).astype(jnp.float32)
        attended = jnp.einsum("hrk,kd->rhd", probs_low, value_tile)
        row_delta = jnp.sum(g_rows * attended, axis=-1)
        grad_prob = jnp.einsum("rhd,kd->hrk", g_rows, value_tile)
        dscore = probs * (grad_prob - jnp.transpose(row_delta)[..., None])
        dscore = lax.optimization_barrier(dscore.astype(jnp.bfloat16)).astype(jnp.float32)
        grad_q = jnp.einsum("hrk,kd->rhd", dscore, key_tile) * scaling
        grad_k = jnp.einsum("hrk,rhd->kd", dscore, q_rows) * scaling
        grad_v = jnp.einsum("hrk,rhd->kd", probs_low, g_rows)
        grad_key_acc = grad_key_acc.at[head_index, block_ids].add(grad_k.reshape(chosen, BLOCK, HEAD_DIM))
        grad_value_acc = grad_value_acc.at[head_index, block_ids].add(grad_v.reshape(chosen, BLOCK, HEAD_DIM))
        return (grad_key_acc, grad_value_acc), (attended.astype(jnp.bfloat16), grad_q)

    start_acc = jnp.zeros((kv_heads, num_blocks, BLOCK, HEAD_DIM), jnp.float32)
    items = jnp.arange(num_blocks * kv_heads, dtype=jnp.int32)
    (grad_key_acc, grad_value_acc), (outputs, grad_qs) = lax.scan(advance, (start_acc, start_acc), items)
    attn_output = outputs.reshape(num_blocks, kv_heads, BLOCK, group_size, HEAD_DIM).transpose(0, 2, 1, 3, 4).reshape(seq_len, -1)
    grad_queries = grad_qs.reshape(num_blocks, kv_heads, BLOCK, group_size, HEAD_DIM).transpose(0, 2, 1, 3, 4).reshape(seq_len, -1)
    grad_keys = grad_key_acc.transpose(1, 2, 0, 3).reshape(seq_len, kv_heads * HEAD_DIM)
    grad_values = grad_value_acc.transpose(1, 2, 0, 3).reshape(seq_len, kv_heads * HEAD_DIM)
    return attn_output, grad_queries, grad_keys, grad_values
```

```python
import jax
import jax.numpy as jnp
from jax import lax
from jax.sharding import Mesh, PartitionSpec as P

BLOCK = 512
NEGATIVE = -1e30
SWAP = [(0, 1), (1, 0)]


def ordered(own_part, other_part, pair):
    return jnp.where(
        pair == 0,
        jnp.concatenate([own_part, other_part], -1),
        jnp.concatenate([other_part, own_part], -1),
    )


def full_features(own, pair):
    other = lax.ppermute(own, "pair", SWAP)
    half = own.shape[-1] // 2
    return jnp.concatenate(
        [
            ordered(own[..., :half], other[..., :half], pair),
            ordered(own[..., half:], other[..., half:], pair),
        ],
        -1,
    )


def local(queries, key_states, value_states, block_picks, grad_output):
    row_count = queries.shape[0]
    half_dim = key_states.shape[1]
    head_dim = 2 * half_dim
    local_heads = queries.shape[1] // head_dim
    z_count = lax.axis_size("z")
    z_index = lax.axis_index("z")
    core = lax.axis_index("core")
    pair = lax.axis_index("pair")
    num_blocks, _, picked = block_picks.shape
    stripe = row_count // z_count
    scaling = head_dim ** (-0.5)
    group_picks = lax.dynamic_index_in_dim(block_picks, lax.axis_index("grp"), 1, keepdims=False)
    wanted = jnp.arange(num_blocks, dtype=jnp.int32)[:, None] - group_picks
    usable = lax.dynamic_index_in_dim(wanted, z_index, 0, keepdims=False) >= 0
    block_ids = jnp.maximum(wanted, 0).reshape(-1)

    own = jnp.concatenate([key_states, value_states], 1)
    banded = lax.all_to_all(
        own.reshape(z_count, stripe, head_dim), "z", split_axis=0, concat_axis=0, tiled=True
    )
    own_full = full_features(own, pair)
    own_pair = jnp.concatenate([own_full, lax.ppermute(own_full, "core", SWAP)], 0)

    outgoing = jnp.take(banded, block_ids, axis=0).reshape(z_count, picked * stripe, head_dim)
    arrived = lax.all_to_all(outgoing, "z", split_axis=0, concat_axis=0, tiled=True)
    fetched = (
        arrived.reshape(z_count, picked, stripe, head_dim)
        .transpose(1, 0, 2, 3)
        .reshape(picked, row_count, head_dim)
    )
    fetched = full_features(fetched, pair)
    fetched = jnp.concatenate([fetched, lax.ppermute(fetched, "core", SWAP)], 1)
    tiles = jnp.concatenate([own_pair[None], fetched], 0).reshape(-1, 2 * head_dim)
    key_tiles = tiles[:, :head_dim]
    value_tiles = tiles[:, head_dim:]
    key_count = tiles.shape[0]

    q_rows = queries.reshape(row_count, local_heads, head_dim)
    g_rows = grad_output.reshape(row_count, local_heads, head_dim)
    spot = jnp.arange(key_count, dtype=jnp.int32)
    place = spot % BLOCK
    key_place = jnp.where(place < row_count, core, 1 - core) * row_count + place % row_count
    query_place = core * row_count + jnp.arange(row_count, dtype=jnp.int32)
    slot_usable = jnp.concatenate([jnp.ones((1,), bool), usable])[spot // BLOCK]
    allowed = slot_usable[None, :] & (
        (spot >= BLOCK)[None, :] | (key_place[None, :] <= query_place[:, None])
    )
    scores = (
        jnp.einsum("rhd,kd->hrk", q_rows, key_tiles, preferred_element_type=jnp.float32) * scaling
    )
    scores = jnp.where(allowed[None], scores, NEGATIVE)
    row_max = jnp.max(scores, axis=-1, keepdims=True)
    weights = jnp.exp(scores - row_max)
    probs = weights / jnp.sum(weights, axis=-1, keepdims=True)
    probs_low = probs.astype(jnp.bfloat16)
    attended = jnp.einsum(
        "hrk,kd->rhd", probs_low, value_tiles, preferred_element_type=jnp.float32
    )
    attn_output = attended.astype(jnp.bfloat16).reshape(row_count, -1)
    row_delta = jnp.sum(g_rows.astype(jnp.float32) * attended, axis=-1)
    grad_prob = jnp.einsum("rhd,kd->hrk", g_rows, value_tiles, preferred_element_type=jnp.float32)
    dscore = (probs * (grad_prob - jnp.transpose(row_delta)[..., None])).astype(jnp.bfloat16)
    grad_queries = (
        jnp.einsum("hrk,kd->rhd", dscore, key_tiles, preferred_element_type=jnp.float32) * scaling
    ).reshape(row_count, -1)
    grad_k = jnp.einsum("hrk,rhd->kd", dscore, q_rows, preferred_element_type=jnp.float32) * scaling
    grad_v = jnp.einsum("hrk,rhd->kd", probs_low, g_rows, preferred_element_type=jnp.float32)

    grads = jnp.concatenate([grad_k, grad_v], -1).reshape(-1, 2, row_count, 2 * head_dim)
    from_core = lax.ppermute(grads[:, 1].astype(jnp.bfloat16), "core", SWAP)
    grads = grads[:, 0] + from_core.astype(jnp.float32)
    quarters = grads.reshape(-1, row_count, 4, half_dim)
    low = jnp.concatenate([quarters[:, :, 0], quarters[:, :, 2]], -1)
    high = jnp.concatenate([quarters[:, :, 1], quarters[:, :, 3]], -1)
    mine = jnp.where(pair == 0, low, high)
    theirs = jnp.where(pair == 0, high, low).astype(jnp.bfloat16)
    mine = mine + lax.ppermute(theirs, "pair", SWAP).astype(jnp.float32)

    going_out = (
        mine[1:]
        .astype(jnp.bfloat16)
        .reshape(picked, z_count, stripe, head_dim)
        .transpose(1, 0, 2, 3)
        .reshape(z_count, picked * stripe, head_dim)
    )
    landed = lax.all_to_all(going_out, "z", split_axis=0, concat_axis=0, tiled=True)
    member = (
        block_ids[None, :] == jnp.arange(num_blocks, dtype=jnp.int32)[:, None]
    ).astype(jnp.bfloat16)
    summed = jnp.dot(
        member,
        landed.reshape(z_count * picked, stripe * head_dim),
        preferred_element_type=jnp.float32,
    )
    back = summed.astype(jnp.bfloat16).reshape(z_count, stripe, head_dim)
    back = lax.all_to_all(back, "z", split_axis=0, concat_axis=0, tiled=True)
    total = mine[0] + back.reshape(row_count, head_dim).astype(jnp.float32)
    return attn_output, grad_queries, total[:, :half_dim], total[:, half_dim:]


def solution(mesh):
    seq, heads = mesh.devices.shape
    split = Mesh(
        mesh.devices.reshape(seq // 2, 2, heads // 2, 2), ("z", "core", "grp", "pair")
    )
    spec = P(("z", "core"), ("grp", "pair"))
    return jax.shard_map(
        local,
        mesh=split,
        in_specs=(spec, spec, spec, P(), spec),
        out_specs=(spec, spec, spec, spec),
        check_vma=False,
    )
```

```python
import functools

import jax
import jax.numpy as jnp
from jax import lax
from jax.experimental import pallas as pl
from jax.experimental.pallas import tpu as pltpu
from jax.sharding import Mesh, PartitionSpec as P

BLOCK = 512
NEGATIVE = -1e30
SWAP = [(0, 1), (1, 0)]
LOG2_E = 1.4426950408889634
F32 = jnp.float32
BF16 = jnp.bfloat16
NT = (((1,), (1,)), ((), ()))
NN = (((1,), (0,)), ((), ()))
LIMIT = 4 << 20


def offset_of(info, picks, block, slot):
    return picks[(block * info[4] + info[2]) * 2 + slot]


def block_of(info, picks, block, slot):
    return jnp.maximum(block - offset_of(info, picks, block, slot), 0)


def dot(a, b, dims=NN):
    return lax.dot_general(a, b, dims, preferred_element_type=F32)


def first_half(shape):
    return lax.broadcasted_iota(jnp.int32, shape, len(shape) - 1) < shape[-1] // 2


def swap_halves(x):
    return pltpu.roll(x, x.shape[-1] // 2, x.ndim - 1)


def attend(
    heads, picked, info, picks, q_ref, g_ref, own_a, own_b, own_c, own_d, x_ref, y_ref, xc_ref, yc_ref,
    out_ref, dq_ref, own_mine, own_theirs, own_away, mine_ref, theirs_ref, away_ref,
    key_scr, value_scr, key_t, value_t, s_scr, dp_scr, low_scr, ds_scr, q_scr, g_scr, dk_scr, dv_scr,
):
    rows = q_ref.shape[0]
    dim = q_ref.shape[1] // heads
    core, pair = info[0], info[1]
    slots = picked + 1
    keys = slots * BLOCK
    scaling = dim ** (-0.5)
    is_low = pair == 0
    stripes = x_ref.shape[0]
    stripe = rows // stripes

    def split(own, other):
        low = jnp.where(is_low, own, other)
        high = jnp.where(is_low, other, own)
        half = first_half(low.shape)
        return jnp.where(half, low, swap_halves(high)), jnp.where(half, swap_halves(low), high)

    def place(at, own, other):
        k, v = split(own, other)
        key_scr[at : at + rows, :] = k.astype(BF16)
        value_scr[at : at + rows, :] = v.astype(BF16)
        key_t[:, at : at + rows] = k.T.astype(BF16)
        value_t[:, at : at + rows] = v.T.astype(BF16)

    place(0, own_a[...].astype(F32), own_b[...].astype(F32))
    place(rows, own_c[...].astype(F32), own_d[...].astype(F32))
    for half, (a_ref, b_ref) in enumerate(((x_ref, y_ref), (xc_ref, yc_ref))):
        a = a_ref[...].astype(F32).reshape(stripes, picked, stripe, dim)
        b = b_ref[...].astype(F32).reshape(stripes, picked, stripe, dim)
        for j in range(picked):
            place(
                (j + 1) * BLOCK + half * rows,
                a[:, j].reshape(rows, dim),
                b[:, j].reshape(rows, dim),
            )

    spans = [(at, at + rows) for at in range(0, keys, rows)]
    for h in range(heads):
        q = q_ref[:, h * dim : (h + 1) * dim]
        g = g_ref[:, h * dim : (h + 1) * dim]
        q_scr[h * rows : (h + 1) * rows, :] = q
        g_scr[h * rows : (h + 1) * rows, :] = g
        top = None
        for i, (lo, hi) in enumerate(spans):
            s = dot(key_scr[lo:hi, :], q, NT)
            if i == 0:
                s = jnp.where(
                    lax.broadcasted_iota(jnp.int32, s.shape, 0)
                    <= lax.broadcasted_iota(jnp.int32, s.shape, 1),
                    s,
                    NEGATIVE,
                )
            elif i == 1:
                s = jnp.where(core == 1, s, NEGATIVE)
            else:
                s = jnp.where(offset_of(info, picks, info[3], (i - 2) // 2) <= info[3], s, NEGATIVE)
            s_scr[lo:hi, :] = s
            m = jnp.max(s, axis=0, keepdims=True)
            top = m if top is None else jnp.maximum(top, m)
        total = jnp.zeros_like(top)
        delta = jnp.zeros_like(top)
        for lo, hi in spans:
            p = jnp.exp2((s_scr[lo:hi, :] - top) * (scaling * LOG2_E))
            dp = dot(value_scr[lo:hi, :], g, NT)
            s_scr[lo:hi, :] = p
            dp_scr[lo:hi, :] = dp
            total = total + jnp.sum(p, axis=0, keepdims=True)
            delta = delta + jnp.sum(p * dp, axis=0, keepdims=True)
        scale = 1.0 / total
        delta = delta * scale
        for lo, hi in spans:
            p = s_scr[lo:hi, :] * scale
            low_scr[lo:hi, h * rows : (h + 1) * rows] = p.astype(BF16)
            ds_scr[lo:hi, h * rows : (h + 1) * rows] = (p * (dp_scr[lo:hi, :] - delta)).astype(BF16)
        out_t = dot(value_t[...], low_scr[:, h * rows : (h + 1) * rows])
        out_ref[:, h * dim : (h + 1) * dim] = out_t.T.astype(BF16)
        dq_t = dot(key_t[...], ds_scr[:, h * rows : (h + 1) * rows])
        dq_ref[:, h * dim : (h + 1) * dim] = dq_t.T * scaling

    for lo, hi in spans:
        dk_scr[lo:hi, :] = dot(ds_scr[lo:hi, :], q_scr[...]) * scaling
        dv_scr[lo:hi, :] = dot(low_scr[lo:hi, :], g_scr[...])

    def parts(at):
        k, v = dk_scr[at : at + rows, :], dv_scr[at : at + rows, :]
        half = first_half(k.shape)
        low = jnp.where(half, k, swap_halves(v))
        high = jnp.where(half, swap_halves(k), v)
        return jnp.where(is_low, low, high), jnp.where(is_low, high, low)

    own_mine[...], own_theirs[...] = parts(0)
    a, b = parts(rows)
    own_away[0] = a.astype(BF16)
    own_away[1] = b.astype(BF16)
    for half in range(2):
        pairs = [parts((j + 1) * BLOCK + half * rows) for j in range(picked)]
        a, b = (
            jnp.concatenate([p[i].reshape(stripes, stripe, dim) for p in pairs], axis=1)
            for i in range(2)
        )
        if half == 0:
            mine_ref[...] = a
            theirs_ref[...] = b
        else:
            away_ref[0] = a.astype(BF16)
            away_ref[1] = b.astype(BF16)


def call(kernel, name, out_shape, scalars, arrays, scratch=(), limit=LIMIT):
    vmem = pl.BlockSpec(memory_space=pltpu.VMEM)
    smem = pl.BlockSpec(memory_space=pltpu.SMEM)
    return pl.pallas_call(
        kernel,
        out_shape=out_shape,
        in_specs=[smem] * len(scalars) + [vmem] * len(arrays),
        out_specs=jax.tree.map(lambda _: vmem, out_shape),
        scratch_shapes=list(scratch),
        compiler_params=pltpu.CompilerParams(vmem_limit_bytes=limit),
        name=name,
    )(*scalars, *arrays)


def attention(info, picks, q, g, own, fetched):
    rows, width = q.shape
    dim = own[0].shape[1]
    heads = width // dim
    striped = fetched[0].shape
    picked = striped[0] * striped[1] // rows
    keys = (picked + 1) * BLOCK
    shape = jax.ShapeDtypeStruct
    return call(
        functools.partial(attend, heads, picked),
        "attend",
        (
            shape((rows, width), BF16),
            shape((rows, width), F32),
            shape((rows, dim), F32),
            shape((rows, dim), F32),
            shape((2, rows, dim), BF16),
            shape(striped, F32),
            shape(striped, F32),
            shape((2, *striped), BF16),
        ),
        (info, picks),
        (q, g, *own, *fetched),
        (
            pltpu.VMEM((keys, dim), BF16),
            pltpu.VMEM((keys, dim), BF16),
            pltpu.VMEM((dim, keys), BF16),
            pltpu.VMEM((dim, keys), BF16),
            pltpu.VMEM((keys, rows), F32),
            pltpu.VMEM((keys, rows), F32),
            pltpu.VMEM((keys, heads * rows), BF16),
            pltpu.VMEM((keys, heads * rows), BF16),
            pltpu.VMEM((heads * rows, dim), BF16),
            pltpu.VMEM((heads * rows, dim), BF16),
            pltpu.VMEM((keys, dim), F32),
            pltpu.VMEM((keys, dim), F32),
        ),
        28 << 20,
    )


def pack(k_ref, v_ref, own_ref, striped_ref):
    both = jnp.concatenate([k_ref[...].astype(F32), v_ref[...].astype(F32)], 0).T
    own_ref[...] = both.astype(BF16)
    striped_ref[...] = both.reshape(striped_ref.shape).astype(BF16)


def gather(info, picks, banded_ref, out_ref, scr):
    scr[...] = banded_ref[...].astype(F32)
    picked = out_ref.shape[1] // scr.shape[1]
    for d in range(out_ref.shape[0]):
        rows = [scr[block_of(info, picks, d, j)] for j in range(picked)]
        out_ref[d] = jnp.concatenate(rows, 0).astype(BF16)


def scatter(info, picks, landed_ref, out_ref, acc):
    acc[...] = jnp.zeros_like(acc)
    stripe = acc.shape[1]
    for d in range(landed_ref.shape[0]):
        rows = landed_ref[d].astype(F32)
        for j in range(rows.shape[0] // stripe):
            at = block_of(info, picks, d, j)
            acc[at] = acc[at] + rows[j * stripe : (j + 1) * stripe]
    out_ref[...] = acc[...].astype(BF16)


def unpack(mine_ref, got_ref, pair_ref, back_ref, gk_ref, gv_ref):
    total = mine_ref[...] + got_ref[0].astype(F32) + pair_ref[...].astype(F32)
    total = total + back_ref[...].astype(F32).reshape(total.shape)
    both = total.T
    gk_ref[...] = both[: gk_ref.shape[0]]
    gv_ref[...] = both[gk_ref.shape[0] :]


def local(queries, key_states, value_states, block_picks, grad_output):
    row_count = queries.shape[0]
    half_dim = key_states.shape[1]
    head_dim = 2 * half_dim
    z_count = lax.axis_size("z")
    picked = block_picks.shape[2]
    stripe = row_count // z_count
    axes = [lax.axis_index(name) for name in ("core", "pair", "grp", "z")]
    info = jnp.stack(axes + [jnp.int32(lax.axis_size("grp"))]).astype(jnp.int32)
    picks = block_picks.reshape(-1)
    shape = jax.ShapeDtypeStruct
    banded_shape = shape((z_count, stripe, head_dim), BF16)
    striped_shape = shape((z_count, picked * stripe, head_dim), BF16)

    def exchange(x):
        other = lax.ppermute(x, "pair", SWAP)
        other_core = lax.ppermute(x, "core", SWAP)
        both = lax.ppermute(x, ("core", "pair"), [(i, 3 - i) for i in range(4)])
        return x, other, other_core, both

    def across(x):
        return lax.all_to_all(x, "z", split_axis=0, concat_axis=0, tiled=True)

    own, striped = call(
        pack,
        "pack",
        (shape((row_count, head_dim), BF16), banded_shape),
        (),
        (key_states.T, value_states.T),
    )
    banded = across(striped)
    own = exchange(own)
    banded, own = lax.optimization_barrier((banded, own))
    scratch = (pltpu.VMEM(banded_shape.shape, F32),)
    outgoing = call(gather, "gather", striped_shape, (info, picks), (banded,), scratch)
    fetched = exchange(across(outgoing))

    out, grad_queries, own_mine, own_theirs, own_away, mine, theirs, away = attention(
        info, picks, queries, grad_output, own, fetched
    )

    def from_partners(theirs, away):
        got = lax.ppermute(away, "core", SWAP)
        summed = (theirs + got[1].astype(F32)).astype(BF16)
        return got, lax.ppermute(summed, "pair", SWAP)

    got, from_pair = from_partners(theirs, away)
    landed = across((mine + got[0].astype(F32) + from_pair.astype(F32)).astype(BF16))
    got, from_pair = from_partners(own_theirs, own_away)
    landed, got, from_pair = lax.optimization_barrier((landed, got, from_pair))
    back = across(call(scatter, "scatter", banded_shape, (info, picks), (landed,), scratch))
    grad_k, grad_v = call(
        unpack,
        "unpack",
        (shape((half_dim, row_count), F32),) * 2,
        (),
        (own_mine, got, from_pair, back),
    )
    return out, grad_queries, grad_k.T, grad_v.T


def solution(mesh):
    seq, heads = mesh.devices.shape
    split = Mesh(
        mesh.devices.reshape(seq // 2, 2, heads // 2, 2), ("z", "core", "grp", "pair")
    )
    spec = P(("z", "core"), ("grp", "pair"))
    return jax.shard_map(
        local,
        mesh=split,
        in_specs=(spec, spec, spec, P(), spec),
        out_specs=(spec, spec, spec, spec),
        check_vma=False,
    )
```

```python
import functools

import jax
import jax.numpy as jnp
from jax import lax
from jax.experimental import pallas as pl
from jax.experimental.pallas import tpu as pltpu
from jax.sharding import Mesh, PartitionSpec as P

BLOCK = 512
NEGATIVE = -1e30
SWAP = [(0, 1), (1, 0)]
LOG2_E = 1.4426950408889634
F32 = jnp.float32
BF16 = jnp.bfloat16
NT = (((1,), (1,)), ((), ()))
NN = (((1,), (0,)), ((), ()))
LIMIT = 4 << 20


def offset_of(info, picks, block, slot):
    return picks[(block * info[4] + info[2]) * 2 + slot]


def block_of(info, picks, block, slot):
    return jnp.maximum(block - offset_of(info, picks, block, slot), 0)


def dot(a, b, dims=NN):
    return lax.dot_general(a, b, dims, preferred_element_type=F32)


def first_half(shape):
    return lax.broadcasted_iota(jnp.int32, shape, len(shape) - 1) < shape[-1] // 2


def swap_halves(x):
    return pltpu.roll(x, x.shape[-1] // 2, x.ndim - 1)


def split_features(is_low, own, other):
    low = jnp.where(is_low, own, other)
    high = jnp.where(is_low, other, own)
    half = first_half(low.shape)
    return jnp.where(half, low, swap_halves(high)), jnp.where(half, swap_halves(low), high)


def join_features(is_low, k, v):
    half = first_half(k.shape)
    low = jnp.where(half, k, swap_halves(v))
    high = jnp.where(half, swap_halves(k), v)
    return jnp.where(is_low, low, high), jnp.where(is_low, high, low)


def load_tiles(pieces, is_low, key_scr, value_scr, key_t, value_t):
    rows = pieces[0][0].shape[0]
    for i, (own, other) in enumerate(pieces):
        k, v = split_features(is_low, own, other)
        at = slice(i * rows, (i + 1) * rows)
        key_scr[at, :] = k.astype(BF16)
        value_scr[at, :] = v.astype(BF16)
        key_t[:, at] = k.T.astype(BF16)
        value_t[:, at] = v.T.astype(BF16)


def spans_of(ref, rows):
    return [slice(at, at + rows) for at in range(0, ref.shape[0], rows)]


def own_scores(
    heads, info, q_ref, g_ref, own_a, own_b, own_c, own_d,
    p_ref, dp_ref, stats, key_t, value_t, q_all, g_all, key_scr, value_scr,
):
    rows = q_ref.shape[0]
    dim = q_ref.shape[1] // heads
    rate = dim ** (-0.5) * LOG2_E
    pieces = [(own_a, own_b), (own_c, own_d)]
    pieces = [tuple(ref[...].astype(F32) for ref in piece) for piece in pieces]
    load_tiles(pieces, info[1] == 0, key_scr, value_scr, key_t, value_t)
    for h in range(heads):
        q = q_ref[:, h * dim : (h + 1) * dim]
        g = g_ref[:, h * dim : (h + 1) * dim]
        col = slice(h * rows, (h + 1) * rows)
        q_all[col, :] = q
        g_all[col, :] = g
        spans = spans_of(key_scr, rows)
        s = dot(key_scr[spans[0], :], q, NT)
        earlier = lax.broadcasted_iota(jnp.int32, s.shape, 0) <= lax.broadcasted_iota(
            jnp.int32, s.shape, 1
        )
        s = jnp.where(earlier, s, NEGATIVE)
        p_ref[spans[0], col] = s
        top = jnp.max(s, axis=0, keepdims=True)
        s = jnp.where(info[0] == 1, dot(key_scr[spans[1], :], q, NT), NEGATIVE)
        p_ref[spans[1], col] = s
        top = jnp.maximum(top, jnp.max(s, axis=0, keepdims=True))
        total = jnp.zeros_like(top)
        delta = jnp.zeros_like(top)
        for span in spans:
            p = jnp.exp2((p_ref[span, col] - top) * rate)
            dp = dot(value_scr[span, :], g, NT)
            p_ref[span, col] = p
            dp_ref[span, col] = dp
            total = total + jnp.sum(p, axis=0, keepdims=True)
            delta = delta + jnp.sum(p * dp, axis=0, keepdims=True)
        stats[0:1, col] = top
        stats[1:2, col] = total
        stats[2:3, col] = delta


def picked_grads(
    heads, picked, info, picks, q_all, g_all, stats, x_ref, y_ref, xc_ref, yc_ref,
    mine_ref, theirs_ref, away_ref, low_ref, ds_ref, key_t, value_t, merged,
    key_scr, value_scr, s_scr, dp_scr,
):
    rows, dim = q_all.shape[0] // heads, q_all.shape[1]
    scaling = dim ** (-0.5)
    rate = scaling * LOG2_E
    is_low = info[1] == 0
    stripes = x_ref.shape[0]
    stripe = rows // stripes
    halves = [
        [ref[...].astype(F32).reshape(stripes, picked, stripe, dim) for ref in refs]
        for refs in ((x_ref, y_ref), (xc_ref, yc_ref))
    ]
    pieces = [
        tuple(part[:, j].reshape(rows, dim) for part in half) for j in range(picked) for half in halves
    ]
    load_tiles(pieces, is_low, key_scr, value_scr, key_t, value_t)
    spans = spans_of(key_scr, rows)
    for h in range(heads):
        col = slice(h * rows, (h + 1) * rows)
        q, g = q_all[col, :], g_all[col, :]
        own_top = stats[0:1, col]
        top = own_top
        for i, span in enumerate(spans):
            s = dot(key_scr[span, :], q, NT)
            s = jnp.where(offset_of(info, picks, info[3], i // 2) <= info[3], s, NEGATIVE)
            s_scr[span, :] = s
            top = jnp.maximum(top, jnp.max(s, axis=0, keepdims=True))
        shift = jnp.exp2((own_top - top) * rate)
        total = stats[1:2, col] * shift
        delta = stats[2:3, col] * shift
        for span in spans:
            p = jnp.exp2((s_scr[span, :] - top) * rate)
            dp = dot(value_scr[span, :], g, NT)
            s_scr[span, :] = p
            dp_scr[span, :] = dp
            total = total + jnp.sum(p, axis=0, keepdims=True)
            delta = delta + jnp.sum(p * dp, axis=0, keepdims=True)
        scale = 1.0 / total
        delta = delta * scale
        merged[0:1, col] = shift * scale
        merged[1:2, col] = delta
        for span in spans:
            p = s_scr[span, :] * scale
            low_ref[span, col] = p.astype(BF16)
            ds_ref[span, col] = (p * (dp_scr[span, :] - delta)).astype(BF16)
    parts = []
    for span in spans:
        k = dot(ds_ref[span, :], q_all[...]) * scaling
        v = dot(low_ref[span, :], g_all[...])
        parts.append(join_features(is_low, k, v))
    for half in range(2):
        a, b = (
            jnp.concatenate(
                [parts[2 * j + half][i].reshape(stripes, stripe, dim) for j in range(picked)], axis=1
            )
            for i in range(2)
        )
        if half == 0:
            mine_ref[...] = a
            theirs_ref[...] = b
        else:
            away_ref[0] = a.astype(BF16)
            away_ref[1] = b.astype(BF16)


def row_outputs(
    heads, info, q_all, g_all, p_ref, dp_ref, merged, own_kt, own_vt, low_ref, ds_ref, key_t, value_t,
    out_ref, dq_ref, own_mine, own_theirs, own_away, low_scr, ds_scr,
):
    rows, dim = q_all.shape[0] // heads, q_all.shape[1]
    scaling = dim ** (-0.5)
    spans = spans_of(p_ref, rows)
    for h in range(heads):
        lane = slice(h * dim, (h + 1) * dim)
        col = slice(h * rows, (h + 1) * rows)
        scale, delta = merged[0:1, col], merged[1:2, col]
        for span in spans:
            p = p_ref[span, col] * scale
            low_scr[span, col] = p.astype(BF16)
            ds_scr[span, col] = (p * (dp_ref[span, col] - delta)).astype(BF16)
        out_t = dot(own_vt[...], low_scr[:, col]) + dot(value_t[...], low_ref[:, col])
        out_ref[:, lane] = out_t.T.astype(BF16)
        dq_t = dot(own_kt[...], ds_scr[:, col]) + dot(key_t[...], ds_ref[:, col])
        dq_ref[:, lane] = dq_t.T * scaling
    for i, span in enumerate(spans):
        k = dot(ds_scr[span, :], q_all[...]) * scaling
        v = dot(low_scr[span, :], g_all[...])
        a, b = join_features(info[1] == 0, k, v)
        if i == 0:
            own_mine[...] = a
            own_theirs[...] = b
        else:
            own_away[0] = a.astype(BF16)
            own_away[1] = b.astype(BF16)


def call(kernel, name, out_shape, scalars, arrays, scratch=(), limit=LIMIT):
    vmem = pl.BlockSpec(memory_space=pltpu.VMEM)
    smem = pl.BlockSpec(memory_space=pltpu.SMEM)
    return pl.pallas_call(
        kernel,
        out_shape=out_shape,
        in_specs=[smem] * len(scalars) + [vmem] * len(arrays),
        out_specs=jax.tree.map(lambda _: vmem, out_shape),
        scratch_shapes=list(scratch),
        compiler_params=pltpu.CompilerParams(vmem_limit_bytes=limit),
        name=name,
    )(*scalars, *arrays)


def pack(k_ref, v_ref, own_ref, striped_ref):
    both = jnp.concatenate([k_ref[...].astype(F32), v_ref[...].astype(F32)], 0).T
    own_ref[...] = both.astype(BF16)
    striped_ref[...] = both.reshape(striped_ref.shape).astype(BF16)


def gather(info, picks, banded_ref, out_ref, scr):
    scr[...] = banded_ref[...].astype(F32)
    picked = out_ref.shape[1] // scr.shape[1]
    for d in range(out_ref.shape[0]):
        rows = [scr[block_of(info, picks, d, j)] for j in range(picked)]
        out_ref[d] = jnp.concatenate(rows, 0).astype(BF16)


def scatter(info, picks, landed_ref, out_ref, acc):
    acc[...] = jnp.zeros_like(acc)
    stripe = acc.shape[1]
    for d in range(landed_ref.shape[0]):
        rows = landed_ref[d].astype(F32)
        for j in range(rows.shape[0] // stripe):
            at = block_of(info, picks, d, j)
            acc[at] = acc[at] + rows[j * stripe : (j + 1) * stripe]
    out_ref[...] = acc[...].astype(BF16)


def unpack(mine_ref, got_ref, pair_ref, back_ref, gk_ref, gv_ref):
    total = mine_ref[...] + got_ref[0].astype(F32) + pair_ref[...].astype(F32)
    total = total + back_ref[...].astype(F32).reshape(total.shape)
    both = total.T
    gk_ref[...] = both[: gk_ref.shape[0]]
    gv_ref[...] = both[gk_ref.shape[0] :]


def local(queries, key_states, value_states, block_picks, grad_output):
    row_count = queries.shape[0]
    half_dim = key_states.shape[1]
    head_dim = 2 * half_dim
    z_count = lax.axis_size("z")
    picked = block_picks.shape[2]
    stripe = row_count // z_count
    axes = [lax.axis_index(name) for name in ("core", "pair", "grp", "z")]
    info = jnp.stack(axes + [jnp.int32(lax.axis_size("grp"))]).astype(jnp.int32)
    picks = block_picks.reshape(-1)
    shape = jax.ShapeDtypeStruct
    banded_shape = shape((z_count, stripe, head_dim), BF16)
    striped_shape = shape((z_count, picked * stripe, head_dim), BF16)

    def exchange(x):
        other_core = lax.ppermute(x, "core", SWAP)
        both = lax.ppermute(x, ("core", "pair"), [(i, 3 - i) for i in range(4)])
        other = lax.ppermute(x, "pair", SWAP)
        return x, other, other_core, both

    def across(x):
        return lax.all_to_all(x, "z", split_axis=0, concat_axis=0, tiled=True)

    own, striped = call(
        pack,
        "pack",
        (shape((row_count, head_dim), BF16), banded_shape),
        (),
        (key_states.T, value_states.T),
    )
    banded = across(striped)
    scratch = (pltpu.VMEM(banded_shape.shape, F32),)
    outgoing = call(gather, "gather", striped_shape, (info, picks), (banded,), scratch)
    own, outgoing = lax.optimization_barrier((own, outgoing))
    own, fetched = lax.optimization_barrier((exchange(own), across(outgoing)))
    fetched = exchange(fetched)

    heads = queries.shape[1] // head_dim
    wide = heads * row_count
    many = picked * BLOCK
    p, dp, stats, own_kt, own_vt, q_all, g_all = call(
        functools.partial(own_scores, heads),
        "own_scores",
        (
            shape((BLOCK, wide), F32),
            shape((BLOCK, wide), F32),
            shape((8, wide), F32),
            shape((head_dim, BLOCK), BF16),
            shape((head_dim, BLOCK), BF16),
            shape((wide, head_dim), BF16),
            shape((wide, head_dim), BF16),
        ),
        (info,),
        (queries, grad_output, *own),
        (pltpu.VMEM((BLOCK, head_dim), BF16), pltpu.VMEM((BLOCK, head_dim), BF16)),
        12 << 20,
    )
    mine, theirs, away, low, ds, key_t, value_t, merged = call(
        functools.partial(picked_grads, heads, picked),
        "picked_grads",
        (
            shape(striped_shape.shape, F32),
            shape(striped_shape.shape, F32),
            shape((2, *striped_shape.shape), BF16),
            shape((many, wide), BF16),
            shape((many, wide), BF16),
            shape((head_dim, many), BF16),
            shape((head_dim, many), BF16),
            shape((8, wide), F32),
        ),
        (info, picks),
        (q_all, g_all, stats, *fetched),
        (
            pltpu.VMEM((many, head_dim), BF16),
            pltpu.VMEM((many, head_dim), BF16),
            pltpu.VMEM((many, row_count), F32),
            pltpu.VMEM((many, row_count), F32),
        ),
        18 << 20,
    )

    def to_core(away):
        return lax.ppermute(away, "core", SWAP)

    def to_pair(theirs, got):
        return lax.ppermute((theirs + got[1].astype(F32)).astype(BF16), "pair", SWAP)

    got = to_core(away)
    from_pair = to_pair(theirs, got)
    out, grad_queries, own_mine, own_theirs, own_away = call(
        functools.partial(row_outputs, heads),
        "row_outputs",
        (
            shape((row_count, heads * head_dim), BF16),
            shape((row_count, heads * head_dim), F32),
            shape((row_count, head_dim), F32),
            shape((row_count, head_dim), F32),
            shape((2, row_count, head_dim), BF16),
        ),
        (info,),
        (q_all, g_all, p, dp, merged, own_kt, own_vt, low, ds, key_t, value_t),
        (
            pltpu.VMEM((BLOCK, wide), BF16),
            pltpu.VMEM((BLOCK, wide), BF16),
        ),
        18 << 20,
    )
    going_out = (mine + got[0].astype(F32) + from_pair.astype(F32)).astype(BF16)
    going_out, own_away = lax.optimization_barrier((going_out, own_away))
    landed = across(going_out)
    got = to_core(own_away)
    from_pair = to_pair(own_theirs, got)
    landed, got, from_pair = lax.optimization_barrier((landed, got, from_pair))
    back = across(call(scatter, "scatter", banded_shape, (info, picks), (landed,), scratch))
    grad_k, grad_v = call(
        unpack,
        "unpack",
        (shape((half_dim, row_count), F32),) * 2,
        (),
        (own_mine, got, from_pair, back),
    )
    return out, grad_queries, grad_k.T, grad_v.T


def solution(mesh):
    seq, heads = mesh.devices.shape
    split = Mesh(
        mesh.devices.reshape(seq // 2, 2, heads // 2, 2), ("z", "core", "grp", "pair")
    )
    spec = P(("z", "core"), ("grp", "pair"))
    return jax.shard_map(
        local,
        mesh=split,
        in_specs=(spec, spec, spec, P(), spec),
        out_specs=(spec, spec, spec, spec),
        check_vma=False,
    )
```

```python
import functools

import jax
import jax.numpy as jnp
from jax import lax
from jax.experimental import pallas as pl
from jax.experimental.pallas import tpu as pltpu
from jax.sharding import Mesh, PartitionSpec as P

BLOCK = 512
NEGATIVE = -1e30
NO_KEY = -1e4
SWAP = [(0, 1), (1, 0)]
LOG2_E = 1.4426950408889634
F32 = jnp.float32
BF16 = jnp.bfloat16
NT = (((1,), (1,)), ((), ()))
NN = (((1,), (0,)), ((), ()))
LIMIT = 4 << 20


def offset_of(info, picks, block, slot):
    return picks[(block * info[4] + info[2]) * 2 + slot]


def block_of(info, picks, block, slot):
    return jnp.maximum(block - offset_of(info, picks, block, slot), 0)


def dot(a, b, dims=NN):
    return lax.dot_general(a, b, dims, preferred_element_type=F32)


def first_half(shape):
    return lax.broadcasted_iota(jnp.int32, shape, len(shape) - 1) < shape[-1] // 2


def swap_halves(x):
    return pltpu.roll(x, x.shape[-1] // 2, x.ndim - 1)


def split_features(is_low, own, other):
    low = jnp.where(is_low, own, other)
    high = jnp.where(is_low, other, own)
    half = first_half(low.shape)
    return jnp.where(half, low, swap_halves(high)), jnp.where(half, swap_halves(low), high)


def join_features(is_low, k, v):
    half = first_half(k.shape)
    low = jnp.where(half, k, swap_halves(v))
    high = jnp.where(half, swap_halves(k), v)
    return jnp.where(is_low, low, high), jnp.where(is_low, high, low)


def load_tiles(pieces, is_low, key_scr, value_scr):
    rows = pieces[0][0].shape[0]
    for i, (own, other) in enumerate(pieces):
        k, v = split_features(is_low, own, other)
        at = slice(i * rows, (i + 1) * rows)
        key_scr[at, :] = k.astype(BF16)
        value_scr[at, :] = v.astype(BF16)


def spans_of(ref, rows):
    return [slice(at, at + rows) for at in range(0, ref.shape[0], rows)]


def own_scores(
    heads, info, q_all, g_all, own_a, own_b, own_c, own_d,
    p_ref, stats, key_scr, value_scr,
):
    rows, dim = q_all.shape[0] // heads, q_all.shape[1]
    rate = dim ** (-0.5) * LOG2_E
    pieces = [(own_a, own_b), (own_c, own_d)]
    pieces = [tuple(ref[...].astype(F32) for ref in piece) for piece in pieces]
    load_tiles(pieces, info[1] == 0, key_scr, value_scr)
    for h in range(heads):
        col = slice(h * rows, (h + 1) * rows)
        q, g = q_all[col, :], g_all[col, :]
        spans = spans_of(key_scr, rows)
        s = dot(key_scr[spans[0], :], q, NT)
        earlier = lax.broadcasted_iota(jnp.int32, s.shape, 0) <= lax.broadcasted_iota(
            jnp.int32, s.shape, 1
        )
        s = jnp.where(earlier, s, NEGATIVE)
        p_ref[spans[0], col] = s
        top = jnp.max(s, axis=0, keepdims=True)
        s = jnp.where(info[0] == 1, dot(key_scr[spans[1], :], q, NT), NEGATIVE)
        p_ref[spans[1], col] = s
        top = jnp.maximum(top, jnp.max(s, axis=0, keepdims=True))
        total = jnp.zeros_like(top)
        delta = jnp.zeros_like(top)
        for span in spans:
            p = jnp.exp2((p_ref[span, col] - top) * rate)
            dp = dot(value_scr[span, :], g, NT)
            p_ref[span, col] = p
            total = total + jnp.sum(p, axis=0, keepdims=True)
            delta = delta + jnp.sum(p * dp, axis=0, keepdims=True)
        stats[0:1, col] = top
        stats[1:2, col] = total
        stats[2:3, col] = delta


def picked_grads(
    heads, picked, info, picks, q_all, g_all, stats, x_ref, y_ref, xc_ref, yc_ref,
    mine_ref, theirs_ref, away_ref, low_ref, ds_ref, key_scr, value_scr, merged, s_scr, dp_scr,
):
    rows, dim = q_all.shape[0] // heads, q_all.shape[1]
    scaling = dim ** (-0.5)
    rate = scaling * LOG2_E
    is_low = info[1] == 0
    stripes = x_ref.shape[0]
    stripe = rows // stripes
    halves = [
        [ref[...].astype(F32).reshape(stripes, picked, stripe, dim) for ref in refs]
        for refs in ((x_ref, y_ref), (xc_ref, yc_ref))
    ]
    pieces = [
        tuple(part[:, j].reshape(rows, dim) for part in half) for j in range(picked) for half in halves
    ]
    load_tiles(pieces, is_low, key_scr, value_scr)
    spans = spans_of(key_scr, rows)
    usable = [offset_of(info, picks, info[3], i // 2) <= info[3] for i in range(len(spans))]
    for h in range(heads):
        col = slice(h * rows, (h + 1) * rows)
        q, g = q_all[col, :], g_all[col, :]
        own_top = stats[0:1, col]
        top = own_top
        for i, span in enumerate(spans):
            s = dot(key_scr[span, :], q, NT)
            s_scr[span, :] = s
            most = jnp.max(s, axis=0, keepdims=True)
            top = jnp.where(usable[i], jnp.maximum(top, most), top)
        shift = jnp.exp2((own_top - top) * rate)
        total = stats[1:2, col] * shift
        delta = stats[2:3, col] * shift
        for i, span in enumerate(spans):
            slope = jnp.where(usable[i], rate, 0.0)
            floor = jnp.where(usable[i], top * -rate, NO_KEY)
            p = jnp.exp2(s_scr[span, :] * slope + floor)
            dp = dot(value_scr[span, :], g, NT)
            s_scr[span, :] = p
            dp_scr[span, :] = dp
            total = total + jnp.sum(p, axis=0, keepdims=True)
            delta = delta + jnp.sum(p * dp, axis=0, keepdims=True)
        scale = 1.0 / total
        delta = delta * scale
        merged[0:1, col] = shift * scale
        merged[1:2, col] = delta
        for span in spans:
            p = s_scr[span, :] * scale
            low_ref[span, col] = p.astype(BF16)
            ds_ref[span, col] = (p * (dp_scr[span, :] - delta)).astype(BF16)
    parts = []
    for span in spans:
        k = dot(ds_ref[span, :], q_all[...]) * scaling
        v = dot(low_ref[span, :], g_all[...])
        parts.append(join_features(is_low, k, v))
    for half in range(2):
        a, b = (
            jnp.concatenate(
                [parts[2 * j + half][i].reshape(stripes, stripe, dim) for j in range(picked)], axis=1
            )
            for i in range(2)
        )
        if half == 0:
            mine_ref[...] = a
            theirs_ref[...] = b
        else:
            away_ref[0] = a.astype(BF16)
            away_ref[1] = b.astype(BF16)


def row_outputs(
    heads, info, q_all, g_all, p_ref, merged, own_keys, own_values, low_ref, ds_ref, keys, values,
    out_ref, dq_ref, own_mine, own_theirs, own_away, low_scr, ds_scr,
):
    rows, dim = q_all.shape[0] // heads, q_all.shape[1]
    scaling = dim ** (-0.5)
    spans = spans_of(p_ref, rows)
    own_kt, own_vt, key_t, value_t = (ref[...].T for ref in (own_keys, own_values, keys, values))
    for h in range(heads):
        lane = slice(h * dim, (h + 1) * dim)
        col = slice(h * rows, (h + 1) * rows)
        scale, delta = merged[0:1, col], merged[1:2, col]
        for span in spans:
            p = p_ref[span, col] * scale
            dp = dot(own_values[span, :], g_all[col, :], NT)
            low_scr[span, col] = p.astype(BF16)
            ds_scr[span, col] = (p * (dp - delta)).astype(BF16)
        out_t = dot(own_vt, low_scr[:, col]) + dot(value_t, low_ref[:, col])
        out_ref[:, lane] = out_t.T.astype(BF16)
        dq_t = dot(own_kt, ds_scr[:, col]) + dot(key_t, ds_ref[:, col])
        dq_ref[:, lane] = dq_t.T * scaling
    for i, span in enumerate(spans):
        k = dot(ds_scr[span, :], q_all[...]) * scaling
        v = dot(low_scr[span, :], g_all[...])
        a, b = join_features(info[1] == 0, k, v)
        if i == 0:
            own_mine[...] = a
            own_theirs[...] = b
        else:
            own_away[0] = a.astype(BF16)
            own_away[1] = b.astype(BF16)


def call(kernel, name, out_shape, scalars, arrays, scratch=(), limit=LIMIT, space=pltpu.VMEM):
    vmem = pl.BlockSpec(memory_space=pltpu.VMEM)
    smem = pl.BlockSpec(memory_space=pltpu.SMEM)
    return pl.pallas_call(
        kernel,
        out_shape=out_shape,
        in_specs=[smem] * len(scalars) + [pl.BlockSpec(memory_space=space)] * len(arrays),
        out_specs=jax.tree.map(lambda _: vmem, out_shape),
        scratch_shapes=list(scratch),
        compiler_params=pltpu.CompilerParams(vmem_limit_bytes=limit),
        name=name,
    )(*scalars, *arrays)


def pack(k_ref, v_ref, own_ref, striped_ref, k_scr, v_scr, sems):
    copies = [
        pltpu.make_async_copy(k_ref, k_scr, sems.at[0]),
        pltpu.make_async_copy(v_ref, v_scr, sems.at[1]),
    ]
    for copy in copies:
        copy.start()
    for copy in copies:
        copy.wait()
    both = jnp.concatenate([k_scr[...].astype(F32), v_scr[...].astype(F32)], 0).T
    own_ref[...] = both.astype(BF16)
    striped_ref[...] = both.reshape(striped_ref.shape).astype(BF16)


def stack_heads(q_ref, g_ref, q_all, g_all, sems):
    rows, dim = q_ref.shape[0], q_all.shape[1]
    heads = q_all.shape[0] // rows
    copies = [
        pltpu.make_async_copy(
            whole.at[:, pl.ds(h * dim, dim)],
            stacked.at[pl.ds(h * rows, rows), :],
            sems.at[i * heads + h],
        )
        for i, (whole, stacked) in enumerate(((q_ref, q_all), (g_ref, g_all)))
        for h in range(heads)
    ]
    for copy in copies:
        copy.start()
    for copy in copies:
        copy.wait()


def gather(info, picks, banded_ref, out_ref, scr):
    scr[...] = banded_ref[...].astype(F32)
    picked = out_ref.shape[1] // scr.shape[1]
    for d in range(out_ref.shape[0]):
        rows = [scr[block_of(info, picks, d, j)] for j in range(picked)]
        out_ref[d] = jnp.concatenate(rows, 0).astype(BF16)


def scatter(info, picks, landed_ref, out_ref, acc):
    acc[...] = jnp.zeros_like(acc)
    stripe = acc.shape[1]
    for d in range(landed_ref.shape[0]):
        rows = landed_ref[d].astype(F32)
        for j in range(rows.shape[0] // stripe):
            at = block_of(info, picks, d, j)
            acc[at] = acc[at] + rows[j * stripe : (j + 1) * stripe]
    out_ref[...] = acc[...].astype(BF16)


def unpack(mine_ref, got_ref, pair_ref, back_ref, gk_ref, gv_ref):
    total = mine_ref[...] + got_ref[0].astype(F32) + pair_ref[...].astype(F32)
    total = total + back_ref[...].astype(F32).reshape(total.shape)
    both = total.T
    gk_ref[...] = both[: gk_ref.shape[0]]
    gv_ref[...] = both[gk_ref.shape[0] :]


def local(queries, key_states, value_states, block_picks, grad_output):
    row_count = queries.shape[0]
    half_dim = key_states.shape[1]
    head_dim = 2 * half_dim
    z_count = lax.axis_size("z")
    picked = block_picks.shape[2]
    stripe = row_count // z_count
    axes = [lax.axis_index(name) for name in ("core", "pair", "grp", "z")]
    info = jnp.stack(axes + [jnp.int32(lax.axis_size("grp"))]).astype(jnp.int32)
    picks = block_picks.reshape(-1)
    shape = jax.ShapeDtypeStruct
    banded_shape = shape((z_count, stripe, head_dim), BF16)
    striped_shape = shape((z_count, picked * stripe, head_dim), BF16)

    def in_hbm(x):
        return pltpu.with_memory_space_constraint(x, pltpu.HBM)

    def to_pair(x):
        return lax.ppermute(x, "pair", SWAP)

    def to_core(x):
        return lax.ppermute(x, "core", SWAP)

    def across(x):
        return lax.all_to_all(x, "z", split_axis=0, concat_axis=0, tiled=True)

    own, striped = call(
        pack,
        "pack",
        (shape((row_count, head_dim), BF16), banded_shape),
        (),
        tuple(in_hbm(x.T) for x in (key_states, value_states)),
        (
            pltpu.VMEM((half_dim, row_count), BF16),
            pltpu.VMEM((half_dim, row_count), BF16),
            pltpu.SemaphoreType.DMA((2,)),
        ),
        space=pltpu.HBM,
    )
    heads = queries.shape[1] // head_dim
    wide = heads * row_count
    many = picked * BLOCK
    banded = across(striped)
    own_pair = to_pair(own)
    q_all, g_all = call(
        stack_heads,
        "stack_heads",
        (shape((wide, head_dim), BF16),) * 2,
        (),
        tuple(in_hbm(x) for x in (queries, grad_output)),
        (pltpu.SemaphoreType.DMA((2 * heads,)),),
        space=pltpu.HBM,
    )
    banded, own, own_pair, q_all, g_all = lax.optimization_barrier(
        (banded, own, own_pair, q_all, g_all)
    )
    scratch = (pltpu.VMEM(banded_shape.shape, F32),)
    outgoing = call(gather, "gather", striped_shape, (info, picks), (banded,), scratch)
    outgoing, own, own_pair = lax.optimization_barrier((outgoing, own, own_pair))
    fetched = across(outgoing)
    own_block = call(
        functools.partial(own_scores, heads),
        "own_scores",
        (
            shape((BLOCK, wide), F32),
            shape((8, wide), F32),
            shape((BLOCK, head_dim), BF16),
            shape((BLOCK, head_dim), BF16),
        ),
        (info,),
        (q_all, g_all, own, own_pair, to_core(own), to_core(own_pair)),
        limit=6 << 20,
    )
    fetched, (p, stats, own_keys, own_values) = lax.optimization_barrier((fetched, own_block))
    fetched_pair = to_pair(fetched)
    fetched = (fetched, fetched_pair, to_core(fetched), to_core(fetched_pair))
    mine, theirs, away, low, ds, keys, values, merged = call(
        functools.partial(picked_grads, heads, picked),
        "picked_grads",
        (
            shape(striped_shape.shape, F32),
            shape(striped_shape.shape, F32),
            shape((2, *striped_shape.shape), BF16),
            shape((many, wide), BF16),
            shape((many, wide), BF16),
            shape((many, head_dim), BF16),
            shape((many, head_dim), BF16),
            shape((8, wide), F32),
        ),
        (info, picks),
        (q_all, g_all, stats, *fetched),
        (
            pltpu.VMEM((many, row_count), F32),
            pltpu.VMEM((many, row_count), F32),
        ),
        8 << 20,
    )

    def summed(theirs, got):
        return (theirs + got[1].astype(F32)).astype(BF16)

    got = to_core(away)
    from_pair = to_pair(summed(theirs, got))
    out, grad_queries, own_mine, own_theirs, own_away = call(
        functools.partial(row_outputs, heads),
        "row_outputs",
        (
            shape((row_count, heads * head_dim), BF16),
            shape((row_count, heads * head_dim), F32),
            shape((row_count, head_dim), F32),
            shape((row_count, head_dim), F32),
            shape((2, row_count, head_dim), BF16),
        ),
        (info,),
        (q_all, g_all, p, merged, own_keys, own_values, low, ds, keys, values),
        (
            pltpu.VMEM((BLOCK, wide), BF16),
            pltpu.VMEM((BLOCK, wide), BF16),
        ),
        8 << 20,
    )
    going_out = (mine + got[0].astype(F32) + from_pair.astype(F32)).astype(BF16)
    going_out, own_away = lax.optimization_barrier((going_out, own_away))
    landed = across(going_out)
    got = to_core(own_away)
    from_pair = to_pair(summed(own_theirs, got))
    landed, got, from_pair = lax.optimization_barrier((landed, got, from_pair))
    back = across(call(scatter, "scatter", banded_shape, (info, picks), (landed,), scratch))
    grad_k, grad_v = call(
        unpack,
        "unpack",
        (shape((half_dim, row_count), F32),) * 2,
        (),
        (own_mine, got, from_pair, back),
    )
    return out, grad_queries, grad_k.T, grad_v.T


def solution(mesh):
    seq, heads = mesh.devices.shape
    split = Mesh(
        mesh.devices.reshape(seq // 2, 2, heads // 2, 2), ("z", "core", "grp", "pair")
    )
    spec = P(("z", "core"), ("grp", "pair"))
    return jax.shard_map(
        local,
        mesh=split,
        in_specs=(spec, spec, spec, P(), spec),
        out_specs=(spec, spec, spec, spec),
        check_vma=False,
    )
```

```python
import functools

import jax
import jax.numpy as jnp
from jax import lax
from jax.experimental import pallas as pl
from jax.experimental.pallas import tpu as pltpu
from jax.sharding import Mesh, PartitionSpec as P

BLOCK = 512
NEGATIVE = -1e30
NO_KEY = -1e4
SWAP = [(0, 1), (1, 0)]
LOG2_E = 1.4426950408889634
F32 = jnp.float32
BF16 = jnp.bfloat16
NT = (((1,), (1,)), ((), ()))
NN = (((1,), (0,)), ((), ()))
LIMIT = 4 << 20


def first_rank(count):
    return count * 5 // 8


def offset_of(info, picks, block, slot):
    return picks[(block * info[4] + info[2]) * 2 + slot]


def rank_of_pick(info, picks, rank, slot, count):
    first = first_rank(count)
    block = (first + rank) % count
    picked = jnp.maximum(block - offset_of(info, picks, block, slot), 0)
    return jnp.where(picked >= first, picked - first, picked - first + count)


def dot(a, b, dims=NN):
    return lax.dot_general(a, b, dims, preferred_element_type=F32)


def first_half(shape):
    return lax.broadcasted_iota(jnp.int32, shape, len(shape) - 1) < shape[-1] // 2


def swap_halves(x):
    return pltpu.roll(x, x.shape[-1] // 2, x.ndim - 1)


def split_features(is_low, own, other):
    low = jnp.where(is_low, own, other)
    high = jnp.where(is_low, other, own)
    half = first_half(low.shape)
    return jnp.where(half, low, swap_halves(high)), jnp.where(half, swap_halves(low), high)


def join_features(is_low, k, v):
    half = first_half(k.shape)
    low = jnp.where(half, k, swap_halves(v))
    high = jnp.where(half, swap_halves(k), v)
    return jnp.where(is_low, low, high), jnp.where(is_low, high, low)


def load_tiles(pieces, is_low, key_scr, value_scr):
    rows = pieces[0][0].shape[0]
    for i, (own, other) in enumerate(pieces):
        k, v = split_features(is_low, own, other)
        at = slice(i * rows, (i + 1) * rows)
        key_scr[at, :] = k.astype(BF16)
        value_scr[at, :] = v.astype(BF16)


def spans_of(ref, rows):
    return [slice(at, at + rows) for at in range(0, ref.shape[0], rows)]


def own_scores(
    heads, info, q_all, g_all, own_a, own_b, own_c, own_d,
    p_ref, stats, key_scr, value_scr,
):
    rows, dim = q_all.shape[0] // heads, q_all.shape[1]
    rate = dim ** (-0.5) * LOG2_E
    pieces = [(own_a, own_b), (own_c, own_d)]
    pieces = [tuple(ref[...].astype(F32) for ref in piece) for piece in pieces]
    load_tiles(pieces, info[1] == 0, key_scr, value_scr)
    for h in range(heads):
        col = slice(h * rows, (h + 1) * rows)
        q, g = q_all[col, :], g_all[col, :]
        spans = spans_of(key_scr, rows)
        s = dot(key_scr[spans[0], :], q, NT)
        earlier = lax.broadcasted_iota(jnp.int32, s.shape, 0) <= lax.broadcasted_iota(
            jnp.int32, s.shape, 1
        )
        s = jnp.where(earlier, s, NEGATIVE)
        p_ref[spans[0], col] = s
        top = jnp.max(s, axis=0, keepdims=True)
        s = jnp.where(info[0] == 1, dot(key_scr[spans[1], :], q, NT), NEGATIVE)
        p_ref[spans[1], col] = s
        top = jnp.maximum(top, jnp.max(s, axis=0, keepdims=True))
        total = jnp.zeros_like(top)
        delta = jnp.zeros_like(top)
        for span in spans:
            p = jnp.exp2((p_ref[span, col] - top) * rate)
            dp = dot(value_scr[span, :], g, NT)
            p_ref[span, col] = p
            total = total + jnp.sum(p, axis=0, keepdims=True)
            delta = delta + jnp.sum(p * dp, axis=0, keepdims=True)
        stats[0:1, col] = top
        stats[1:2, col] = total
        stats[2:3, col] = delta


def picked_grads(
    heads, picked, info, picks, q_all, g_all, stats, x_ref, y_ref, xc_ref, yc_ref,
    mine_ref, theirs_ref, away_ref, low_ref, ds_ref, key_scr, value_scr, merged, s_scr, dp_scr,
):
    rows, dim = q_all.shape[0] // heads, q_all.shape[1]
    scaling = dim ** (-0.5)
    rate = scaling * LOG2_E
    is_low = info[1] == 0
    stripes = x_ref.shape[0]
    stripe = rows // stripes
    halves = [
        [ref[...].astype(F32).reshape(stripes, picked, stripe, dim) for ref in refs]
        for refs in ((x_ref, y_ref), (xc_ref, yc_ref))
    ]
    pieces = [
        tuple(part[:, j].reshape(rows, dim) for part in half) for j in range(picked) for half in halves
    ]
    load_tiles(pieces, is_low, key_scr, value_scr)
    spans = spans_of(key_scr, rows)
    usable = [offset_of(info, picks, info[3], i // 2) <= info[3] for i in range(len(spans))]
    for h in range(heads):
        col = slice(h * rows, (h + 1) * rows)
        q, g = q_all[col, :], g_all[col, :]
        own_top = stats[0:1, col]
        top = own_top
        for i, span in enumerate(spans):
            s = dot(key_scr[span, :], q, NT)
            s_scr[span, :] = s
            most = jnp.max(s, axis=0, keepdims=True)
            top = jnp.where(usable[i], jnp.maximum(top, most), top)
        shift = jnp.exp2((own_top - top) * rate)
        total = stats[1:2, col] * shift
        delta = stats[2:3, col] * shift
        for i, span in enumerate(spans):
            slope = jnp.where(usable[i], rate, 0.0)
            floor = jnp.where(usable[i], top * -rate, NO_KEY)
            p = jnp.exp2(s_scr[span, :] * slope + floor)
            dp = dot(value_scr[span, :], g, NT)
            s_scr[span, :] = p
            dp_scr[span, :] = dp
            total = total + jnp.sum(p, axis=0, keepdims=True)
            delta = delta + jnp.sum(p * dp, axis=0, keepdims=True)
        scale = 1.0 / total
        delta = delta * scale
        merged[0:1, col] = shift * scale
        merged[1:2, col] = delta
        for span in spans:
            p = s_scr[span, :] * scale
            low_ref[span, col] = p.astype(BF16)
            ds_ref[span, col] = (p * (dp_scr[span, :] - delta)).astype(BF16)
    parts = []
    for span in spans:
        k = dot(ds_ref[span, :], q_all[...]) * scaling
        v = dot(low_ref[span, :], g_all[...])
        parts.append(join_features(is_low, k, v))
    for half in range(2):
        a, b = (
            jnp.concatenate(
                [parts[2 * j + half][i].reshape(stripes, stripe, dim) for j in range(picked)], axis=1
            )
            for i in range(2)
        )
        if half == 0:
            mine_ref[...] = a
            theirs_ref[...] = b
        else:
            away_ref[0] = a.astype(BF16)
            away_ref[1] = b.astype(BF16)


def row_outputs(
    heads, info, q_all, g_all, p_ref, merged, own_keys, own_values, low_ref, ds_ref, keys, values,
    out_ref, dq_ref, own_mine, own_theirs, own_away, low_scr, ds_scr,
):
    rows, dim = q_all.shape[0] // heads, q_all.shape[1]
    scaling = dim ** (-0.5)
    spans = spans_of(p_ref, rows)
    own_kt, own_vt, key_t, value_t = (ref[...].T for ref in (own_keys, own_values, keys, values))
    for h in range(heads):
        lane = slice(h * dim, (h + 1) * dim)
        col = slice(h * rows, (h + 1) * rows)
        scale, delta = merged[0:1, col], merged[1:2, col]
        for span in spans:
            p = p_ref[span, col] * scale
            dp = dot(own_values[span, :], g_all[col, :], NT)
            low_scr[span, col] = p.astype(BF16)
            ds_scr[span, col] = (p * (dp - delta)).astype(BF16)
        out_t = dot(own_vt, low_scr[:, col]) + dot(value_t, low_ref[:, col])
        out_ref[:, lane] = out_t.T.astype(BF16)
        dq_t = dot(own_kt, ds_scr[:, col]) + dot(key_t, ds_ref[:, col])
        dq_ref[:, lane] = dq_t.T * scaling
    for i, span in enumerate(spans):
        k = dot(ds_scr[span, :], q_all[...]) * scaling
        v = dot(low_scr[span, :], g_all[...])
        a, b = join_features(info[1] == 0, k, v)
        if i == 0:
            own_mine[...] = a
            own_theirs[...] = b
        else:
            own_away[0] = a.astype(BF16)
            own_away[1] = b.astype(BF16)


def call(kernel, name, out_shape, scalars, arrays, scratch=(), limit=LIMIT, space=pltpu.VMEM):
    vmem = pl.BlockSpec(memory_space=pltpu.VMEM)
    smem = pl.BlockSpec(memory_space=pltpu.SMEM)
    return pl.pallas_call(
        kernel,
        out_shape=out_shape,
        in_specs=[smem] * len(scalars) + [pl.BlockSpec(memory_space=space)] * len(arrays),
        out_specs=jax.tree.map(lambda _: vmem, out_shape),
        scratch_shapes=list(scratch),
        compiler_params=pltpu.CompilerParams(vmem_limit_bytes=limit),
        name=name,
    )(*scalars, *arrays)


def pack(k_ref, v_ref, own_ref, striped_ref, k_scr, v_scr, sems):
    copies = [
        pltpu.make_async_copy(k_ref, k_scr, sems.at[0]),
        pltpu.make_async_copy(v_ref, v_scr, sems.at[1]),
    ]
    for copy in copies:
        copy.start()
    for copy in copies:
        copy.wait()
    both = jnp.concatenate([k_scr[...].astype(F32), v_scr[...].astype(F32)], 0).T
    own_ref[...] = both.astype(BF16)
    striped_ref[...] = both.reshape(striped_ref.shape).astype(BF16)


def stack_heads(q_ref, g_ref, q_all, g_all, sems):
    rows, dim = q_ref.shape[0], q_all.shape[1]
    heads = q_all.shape[0] // rows
    copies = [
        pltpu.make_async_copy(
            whole.at[:, pl.ds(h * dim, dim)],
            stacked.at[pl.ds(h * rows, rows), :],
            sems.at[i * heads + h],
        )
        for i, (whole, stacked) in enumerate(((q_ref, q_all), (g_ref, g_all)))
        for h in range(heads)
    ]
    for copy in copies:
        copy.start()
    for copy in copies:
        copy.wait()


def gather(info, picks, banded_ref, out_ref, scr):
    scr[...] = banded_ref[...].astype(F32)
    picked = out_ref.shape[1] // scr.shape[1]
    count = out_ref.shape[0]
    for rank in range(count):
        rows = [scr[rank_of_pick(info, picks, rank, j, count)] for j in range(picked)]
        out_ref[rank] = jnp.concatenate(rows, 0).astype(BF16)


def scatter(info, picks, landed_ref, out_ref, acc):
    acc[...] = jnp.zeros_like(acc)
    stripe = acc.shape[1]
    count = landed_ref.shape[0]
    for rank in range(count):
        rows = landed_ref[rank].astype(F32)
        for j in range(rows.shape[0] // stripe):
            at = rank_of_pick(info, picks, rank, j, count)
            acc[at] = acc[at] + rows[j * stripe : (j + 1) * stripe]
    out_ref[...] = acc[...].astype(BF16)


def unpack(mine_ref, got_ref, pair_ref, back_ref, gk_ref, gv_ref):
    total = mine_ref[...] + got_ref[0].astype(F32) + pair_ref[...].astype(F32)
    total = total + back_ref[...].astype(F32).reshape(total.shape)
    both = total.T
    gk_ref[...] = both[: gk_ref.shape[0]]
    gv_ref[...] = both[gk_ref.shape[0] :]


def local(queries, key_states, value_states, block_picks, grad_output):
    row_count = queries.shape[0]
    half_dim = key_states.shape[1]
    head_dim = 2 * half_dim
    z_count = lax.axis_size("z")
    picked = block_picks.shape[2]
    stripe = row_count // z_count
    axes = [lax.axis_index(name) for name in ("core", "pair", "grp", "z")]
    info = jnp.stack(axes + [jnp.int32(lax.axis_size("grp"))]).astype(jnp.int32)
    picks = block_picks.reshape(-1)
    shape = jax.ShapeDtypeStruct
    banded_shape = shape((z_count, stripe, head_dim), BF16)
    striped_shape = shape((z_count, picked * stripe, head_dim), BF16)

    def in_hbm(x):
        return pltpu.with_memory_space_constraint(x, pltpu.HBM)

    def to_pair(x):
        return lax.ppermute(x, "pair", SWAP)

    def to_core(x):
        return lax.ppermute(x, "core", SWAP)

    def across(x):
        order = [(first_rank(z_count) + i) % z_count for i in range(z_count)]
        return lax.all_to_all(
            x, "z", split_axis=0, concat_axis=0, axis_index_groups=[order], tiled=True
        )

    own, striped = call(
        pack,
        "pack",
        (shape((row_count, head_dim), BF16), banded_shape),
        (),
        tuple(in_hbm(x.T) for x in (key_states, value_states)),
        (
            pltpu.VMEM((half_dim, row_count), BF16),
            pltpu.VMEM((half_dim, row_count), BF16),
            pltpu.SemaphoreType.DMA((2,)),
        ),
        space=pltpu.HBM,
    )
    heads = queries.shape[1] // head_dim
    wide = heads * row_count
    many = picked * BLOCK
    banded = across(striped)
    own_pair = to_pair(own)
    q_all, g_all = call(
        stack_heads,
        "stack_heads",
        (shape((wide, head_dim), BF16),) * 2,
        (),
        tuple(in_hbm(x) for x in (queries, grad_output)),
        (pltpu.SemaphoreType.DMA((2 * heads,)),),
        space=pltpu.HBM,
    )
    banded, own, own_pair, q_all, g_all = lax.optimization_barrier(
        (banded, own, own_pair, q_all, g_all)
    )
    scratch = (pltpu.VMEM(banded_shape.shape, F32),)
    outgoing = call(gather, "gather", striped_shape, (info, picks), (banded,), scratch)
    outgoing, own, own_pair = lax.optimization_barrier((outgoing, own, own_pair))
    fetched = across(outgoing)
    own_block = call(
        functools.partial(own_scores, heads),
        "own_scores",
        (
            shape((BLOCK, wide), F32),
            shape((8, wide), F32),
            shape((BLOCK, head_dim), BF16),
            shape((BLOCK, head_dim), BF16),
        ),
        (info,),
        (q_all, g_all, own, own_pair, to_core(own), to_core(own_pair)),
        limit=6 << 20,
    )
    fetched, (p, stats, own_keys, own_values) = lax.optimization_barrier((fetched, own_block))
    fetched_pair = to_pair(fetched)
    fetched = (fetched, fetched_pair, to_core(fetched), to_core(fetched_pair))
    mine, theirs, away, low, ds, keys, values, merged = call(
        functools.partial(picked_grads, heads, picked),
        "picked_grads",
        (
            shape(striped_shape.shape, F32),
            shape(striped_shape.shape, F32),
            shape((2, *striped_shape.shape), BF16),
            shape((many, wide), BF16),
            shape((many, wide), BF16),
            shape((many, head_dim), BF16),
            shape((many, head_dim), BF16),
            shape((8, wide), F32),
        ),
        (info, picks),
        (q_all, g_all, stats, *fetched),
        (
            pltpu.VMEM((many, row_count), F32),
            pltpu.VMEM((many, row_count), F32),
        ),
        8 << 20,
    )

    def summed(theirs, got):
        return (theirs + got[1].astype(F32)).astype(BF16)

    got = to_core(away)
    from_pair = to_pair(summed(theirs, got))
    out, grad_queries, own_mine, own_theirs, own_away = call(
        functools.partial(row_outputs, heads),
        "row_outputs",
        (
            shape((row_count, heads * head_dim), BF16),
            shape((row_count, heads * head_dim), F32),
            shape((row_count, head_dim), F32),
            shape((row_count, head_dim), F32),
            shape((2, row_count, head_dim), BF16),
        ),
        (info,),
        (q_all, g_all, p, merged, own_keys, own_values, low, ds, keys, values),
        (
            pltpu.VMEM((BLOCK, wide), BF16),
            pltpu.VMEM((BLOCK, wide), BF16),
        ),
        8 << 20,
    )
    going_out = (mine + got[0].astype(F32) + from_pair.astype(F32)).astype(BF16)
    going_out, own_away = lax.optimization_barrier((going_out, own_away))
    landed = across(going_out)
    got = to_core(own_away)
    from_pair = to_pair(summed(own_theirs, got))
    landed, got, from_pair = lax.optimization_barrier((landed, got, from_pair))
    back = across(call(scatter, "scatter", banded_shape, (info, picks), (landed,), scratch))
    grad_k, grad_v = call(
        unpack,
        "unpack",
        (shape((half_dim, row_count), F32),) * 2,
        (),
        (own_mine, got, from_pair, back),
    )
    return out, grad_queries, grad_k.T, grad_v.T


def solution(mesh):
    seq, heads = mesh.devices.shape
    split = Mesh(
        mesh.devices.reshape(seq // 2, 2, heads // 2, 2), ("z", "core", "grp", "pair")
    )
    spec = P(("z", "core"), ("grp", "pair"))
    return jax.shard_map(
        local,
        mesh=split,
        in_specs=(spec, spec, spec, P(), spec),
        out_specs=(spec, spec, spec, spec),
        check_vma=False,
    )
```

```python
import functools

import jax
import jax.numpy as jnp
from jax import lax
from jax.experimental import pallas as pl
from jax.experimental.pallas import tpu as pltpu
from jax.sharding import Mesh, PartitionSpec as P

BLOCK = 512
NEGATIVE = -1e30
NO_KEY = -1e4
SWAP = [(0, 1), (1, 0)]
LOG2_E = 1.4426950408889634
F32 = jnp.float32
BF16 = jnp.bfloat16
NT = (((1,), (1,)), ((), ()))
NN = (((1,), (0,)), ((), ()))
LIMIT = 4 << 20


def first_rank(count):
    return count * 5 // 8


def stride_of(count):
    return count // 2 - 1


def offset_of(info, picks, block, slot):
    return picks[(block * info[4] + info[2]) * 2 + slot]


def rank_of_pick(info, picks, rank, slot, count):
    first = first_rank(count)
    block = (first + stride_of(count) * rank) % count
    picked = jnp.maximum(block - offset_of(info, picks, block, slot), 0)
    return lax.rem((picked - first + count) * stride_of(count), count)


def dot(a, b, dims=NN):
    return lax.dot_general(a, b, dims, preferred_element_type=F32)


def first_half(shape):
    return lax.broadcasted_iota(jnp.int32, shape, len(shape) - 1) < shape[-1] // 2


def swap_halves(x):
    return pltpu.roll(x, x.shape[-1] // 2, x.ndim - 1)


def split_features(is_low, own, other):
    low = jnp.where(is_low, own, other)
    high = jnp.where(is_low, other, own)
    half = first_half(low.shape)
    return jnp.where(half, low, swap_halves(high)), jnp.where(half, swap_halves(low), high)


def join_features(is_low, k, v):
    half = first_half(k.shape)
    low = jnp.where(half, k, swap_halves(v))
    high = jnp.where(half, swap_halves(k), v)
    return jnp.where(is_low, low, high), jnp.where(is_low, high, low)


def load_tiles(pieces, is_low, key_scr, value_scr):
    rows = pieces[0][0].shape[0]
    for i, (own, other) in enumerate(pieces):
        k, v = split_features(is_low, own, other)
        at = slice(i * rows, (i + 1) * rows)
        key_scr[at, :] = k.astype(BF16)
        value_scr[at, :] = v.astype(BF16)


def spans_of(ref, rows):
    return [slice(at, at + rows) for at in range(0, ref.shape[0], rows)]


def own_scores(
    heads, info, q_all, g_all, own_a, own_b, own_c, own_d,
    p_ref, stats, key_scr, value_scr,
):
    rows, dim = q_all.shape[0] // heads, q_all.shape[1]
    rate = dim ** (-0.5) * LOG2_E
    pieces = [(own_a, own_b), (own_c, own_d)]
    pieces = [tuple(ref[...].astype(F32) for ref in piece) for piece in pieces]
    load_tiles(pieces, info[1] == 0, key_scr, value_scr)
    for h in range(heads):
        col = slice(h * rows, (h + 1) * rows)
        q, g = q_all[col, :], g_all[col, :]
        spans = spans_of(key_scr, rows)
        s = dot(key_scr[spans[0], :], q, NT)
        earlier = lax.broadcasted_iota(jnp.int32, s.shape, 0) <= lax.broadcasted_iota(
            jnp.int32, s.shape, 1
        )
        s = jnp.where(earlier, s, NEGATIVE)
        p_ref[spans[0], col] = s
        top = jnp.max(s, axis=0, keepdims=True)
        s = jnp.where(info[0] == 1, dot(key_scr[spans[1], :], q, NT), NEGATIVE)
        p_ref[spans[1], col] = s
        top = jnp.maximum(top, jnp.max(s, axis=0, keepdims=True))
        total = jnp.zeros_like(top)
        delta = jnp.zeros_like(top)
        for span in spans:
            p = jnp.exp2((p_ref[span, col] - top) * rate)
            dp = dot(value_scr[span, :], g, NT)
            p_ref[span, col] = p
            total = total + jnp.sum(p, axis=0, keepdims=True)
            delta = delta + jnp.sum(p * dp, axis=0, keepdims=True)
        stats[0:1, col] = top
        stats[1:2, col] = total
        stats[2:3, col] = delta


def picked_grads(
    heads, picked, info, picks, q_all, g_all, stats, x_ref, y_ref, xc_ref, yc_ref,
    mine_ref, theirs_ref, away_ref, low_ref, ds_ref, key_scr, value_scr, merged, s_scr, dp_scr,
):
    rows, dim = q_all.shape[0] // heads, q_all.shape[1]
    scaling = dim ** (-0.5)
    rate = scaling * LOG2_E
    is_low = info[1] == 0
    stripes = x_ref.shape[0]
    stripe = rows // stripes
    halves = [
        [ref[...].astype(F32).reshape(stripes, picked, stripe, dim) for ref in refs]
        for refs in ((x_ref, y_ref), (xc_ref, yc_ref))
    ]
    pieces = [
        tuple(part[:, j].reshape(rows, dim) for part in half) for j in range(picked) for half in halves
    ]
    load_tiles(pieces, is_low, key_scr, value_scr)
    spans = spans_of(key_scr, rows)
    usable = [offset_of(info, picks, info[3], i // 2) <= info[3] for i in range(len(spans))]
    for h in range(heads):
        col = slice(h * rows, (h + 1) * rows)
        q, g = q_all[col, :], g_all[col, :]
        own_top = stats[0:1, col]
        top = own_top
        for i, span in enumerate(spans):
            s = dot(key_scr[span, :], q, NT)
            s_scr[span, :] = s
            most = jnp.max(s, axis=0, keepdims=True)
            top = jnp.where(usable[i], jnp.maximum(top, most), top)
        shift = jnp.exp2((own_top - top) * rate)
        total = stats[1:2, col] * shift
        delta = stats[2:3, col] * shift
        for i, span in enumerate(spans):
            slope = jnp.where(usable[i], rate, 0.0)
            floor = jnp.where(usable[i], top * -rate, NO_KEY)
            p = jnp.exp2(s_scr[span, :] * slope + floor)
            dp = dot(value_scr[span, :], g, NT)
            s_scr[span, :] = p
            dp_scr[span, :] = dp
            total = total + jnp.sum(p, axis=0, keepdims=True)
            delta = delta + jnp.sum(p * dp, axis=0, keepdims=True)
        scale = 1.0 / total
        delta = delta * scale
        merged[0:1, col] = shift * scale
        merged[1:2, col] = delta
        for span in spans:
            p = s_scr[span, :] * scale
            low_ref[span, col] = p.astype(BF16)
            ds_ref[span, col] = (p * (dp_scr[span, :] - delta)).astype(BF16)
    parts = []
    for span in spans:
        k = dot(ds_ref[span, :], q_all[...]) * scaling
        v = dot(low_ref[span, :], g_all[...])
        parts.append(join_features(is_low, k, v))
    for half in range(2):
        a, b = (
            jnp.concatenate(
                [parts[2 * j + half][i].reshape(stripes, stripe, dim) for j in range(picked)], axis=1
            )
            for i in range(2)
        )
        if half == 0:
            mine_ref[...] = a
            theirs_ref[...] = b
        else:
            away_ref[0] = a.astype(BF16)
            away_ref[1] = b.astype(BF16)


def row_outputs(
    heads, info, q_all, g_all, p_ref, merged, own_keys, own_values, low_ref, ds_ref, keys, values,
    out_ref, dq_ref, own_mine, own_theirs, own_away, low_scr, ds_scr,
):
    rows, dim = q_all.shape[0] // heads, q_all.shape[1]
    scaling = dim ** (-0.5)
    spans = spans_of(p_ref, rows)
    own_kt, own_vt, key_t, value_t = (ref[...].T for ref in (own_keys, own_values, keys, values))
    for h in range(heads):
        lane = slice(h * dim, (h + 1) * dim)
        col = slice(h * rows, (h + 1) * rows)
        scale, delta = merged[0:1, col], merged[1:2, col]
        for span in spans:
            p = p_ref[span, col] * scale
            dp = dot(own_values[span, :], g_all[col, :], NT)
            low_scr[span, col] = p.astype(BF16)
            ds_scr[span, col] = (p * (dp - delta)).astype(BF16)
        out_t = dot(own_vt, low_scr[:, col]) + dot(value_t, low_ref[:, col])
        out_ref[:, lane] = out_t.T.astype(BF16)
        dq_t = dot(own_kt, ds_scr[:, col]) + dot(key_t, ds_ref[:, col])
        dq_ref[:, lane] = dq_t.T * scaling
    for i, span in enumerate(spans):
        k = dot(ds_scr[span, :], q_all[...]) * scaling
        v = dot(low_scr[span, :], g_all[...])
        a, b = join_features(info[1] == 0, k, v)
        if i == 0:
            own_mine[...] = a
            own_theirs[...] = b
        else:
            own_away[0] = a.astype(BF16)
            own_away[1] = b.astype(BF16)


def call(kernel, name, out_shape, scalars, arrays, scratch=(), limit=LIMIT, space=pltpu.VMEM):
    vmem = pl.BlockSpec(memory_space=pltpu.VMEM)
    smem = pl.BlockSpec(memory_space=pltpu.SMEM)
    return pl.pallas_call(
        kernel,
        out_shape=out_shape,
        in_specs=[smem] * len(scalars) + [pl.BlockSpec(memory_space=space)] * len(arrays),
        out_specs=jax.tree.map(lambda _: vmem, out_shape),
        scratch_shapes=list(scratch),
        compiler_params=pltpu.CompilerParams(vmem_limit_bytes=limit),
        name=name,
    )(*scalars, *arrays)


def pack(k_ref, v_ref, own_ref, striped_ref, k_scr, v_scr, sems):
    copies = [
        pltpu.make_async_copy(k_ref, k_scr, sems.at[0]),
        pltpu.make_async_copy(v_ref, v_scr, sems.at[1]),
    ]
    for copy in copies:
        copy.start()
    for copy in copies:
        copy.wait()
    both = jnp.concatenate([k_scr[...].astype(F32), v_scr[...].astype(F32)], 0).T
    own_ref[...] = both.astype(BF16)
    striped_ref[...] = both.reshape(striped_ref.shape).astype(BF16)


def stack_heads(q_ref, g_ref, q_all, g_all, sems):
    rows, dim = q_ref.shape[0], q_all.shape[1]
    heads = q_all.shape[0] // rows
    copies = [
        pltpu.make_async_copy(
            whole.at[:, pl.ds(h * dim, dim)],
            stacked.at[pl.ds(h * rows, rows), :],
            sems.at[i * heads + h],
        )
        for i, (whole, stacked) in enumerate(((q_ref, q_all), (g_ref, g_all)))
        for h in range(heads)
    ]
    for copy in copies:
        copy.start()
    for copy in copies:
        copy.wait()


def gather(info, picks, banded_ref, out_ref, scr):
    scr[...] = banded_ref[...].astype(F32)
    picked = out_ref.shape[1] // scr.shape[1]
    count = out_ref.shape[0]
    for rank in range(count):
        rows = [scr[rank_of_pick(info, picks, rank, j, count)] for j in range(picked)]
        out_ref[rank] = jnp.concatenate(rows, 0).astype(BF16)


def scatter(info, picks, landed_ref, out_ref, acc):
    acc[...] = jnp.zeros_like(acc)
    stripe = acc.shape[1]
    count = landed_ref.shape[0]
    for rank in range(count):
        rows = landed_ref[rank].astype(F32)
        for j in range(rows.shape[0] // stripe):
            at = rank_of_pick(info, picks, rank, j, count)
            acc[at] = acc[at] + rows[j * stripe : (j + 1) * stripe]
    out_ref[...] = acc[...].astype(BF16)


def unpack(mine_ref, got_ref, pair_ref, back_ref, gk_ref, gv_ref):
    total = mine_ref[...] + got_ref[0].astype(F32) + pair_ref[...].astype(F32)
    total = total + back_ref[...].astype(F32).reshape(total.shape)
    both = total.T
    gk_ref[...] = both[: gk_ref.shape[0]]
    gv_ref[...] = both[gk_ref.shape[0] :]


def local(queries, key_states, value_states, block_picks, grad_output):
    row_count = queries.shape[0]
    half_dim = key_states.shape[1]
    head_dim = 2 * half_dim
    z_count = lax.axis_size("z")
    picked = block_picks.shape[2]
    stripe = row_count // z_count
    axes = [lax.axis_index(name) for name in ("core", "pair", "grp", "z")]
    info = jnp.stack(axes + [jnp.int32(lax.axis_size("grp"))]).astype(jnp.int32)
    picks = block_picks.reshape(-1)
    shape = jax.ShapeDtypeStruct
    banded_shape = shape((z_count, stripe, head_dim), BF16)
    striped_shape = shape((z_count, picked * stripe, head_dim), BF16)

    def in_hbm(x):
        return pltpu.with_memory_space_constraint(x, pltpu.HBM)

    def to_pair(x):
        return lax.ppermute(x, "pair", SWAP)

    def to_core(x):
        return lax.ppermute(x, "core", SWAP)

    def across(x):
        first, stride = first_rank(z_count), stride_of(z_count)
        order = [(first + stride * i) % z_count for i in range(z_count)]
        return lax.all_to_all(
            x, "z", split_axis=0, concat_axis=0, axis_index_groups=[order], tiled=True
        )

    own, striped = call(
        pack,
        "pack",
        (shape((row_count, head_dim), BF16), banded_shape),
        (),
        tuple(in_hbm(x.T) for x in (key_states, value_states)),
        (
            pltpu.VMEM((half_dim, row_count), BF16),
            pltpu.VMEM((half_dim, row_count), BF16),
            pltpu.SemaphoreType.DMA((2,)),
        ),
        space=pltpu.HBM,
    )
    heads = queries.shape[1] // head_dim
    wide = heads * row_count
    many = picked * BLOCK
    banded = across(striped)
    own_pair = to_pair(own)
    q_all, g_all = call(
        stack_heads,
        "stack_heads",
        (shape((wide, head_dim), BF16),) * 2,
        (),
        tuple(in_hbm(x) for x in (queries, grad_output)),
        (pltpu.SemaphoreType.DMA((2 * heads,)),),
        space=pltpu.HBM,
    )
    banded, own, own_pair, q_all, g_all = lax.optimization_barrier(
        (banded, own, own_pair, q_all, g_all)
    )
    scratch = (pltpu.VMEM(banded_shape.shape, F32),)
    outgoing = call(gather, "gather", striped_shape, (info, picks), (banded,), scratch)
    outgoing, own, own_pair = lax.optimization_barrier((outgoing, own, own_pair))
    fetched = across(outgoing)
    own_block = call(
        functools.partial(own_scores, heads),
        "own_scores",
        (
            shape((BLOCK, wide), F32),
            shape((8, wide), F32),
            shape((BLOCK, head_dim), BF16),
            shape((BLOCK, head_dim), BF16),
        ),
        (info,),
        (q_all, g_all, own, own_pair, to_core(own), to_core(own_pair)),
        limit=6 << 20,
    )
    fetched, (p, stats, own_keys, own_values) = lax.optimization_barrier((fetched, own_block))
    fetched_pair = to_pair(fetched)
    fetched = (fetched, fetched_pair, to_core(fetched), to_core(fetched_pair))
    mine, theirs, away, low, ds, keys, values, merged = call(
        functools.partial(picked_grads, heads, picked),
        "picked_grads",
        (
            shape(striped_shape.shape, F32),
            shape(striped_shape.shape, F32),
            shape((2, *striped_shape.shape), BF16),
            shape((many, wide), BF16),
            shape((many, wide), BF16),
            shape((many, head_dim), BF16),
            shape((many, head_dim), BF16),
            shape((8, wide), F32),
        ),
        (info, picks),
        (q_all, g_all, stats, *fetched),
        (
            pltpu.VMEM((many, row_count), F32),
            pltpu.VMEM((many, row_count), F32),
        ),
        8 << 20,
    )

    def summed(theirs, got):
        return (theirs + got[1].astype(F32)).astype(BF16)

    got = to_core(away)
    from_pair = to_pair(summed(theirs, got))
    out, grad_queries, own_mine, own_theirs, own_away = call(
        functools.partial(row_outputs, heads),
        "row_outputs",
        (
            shape((row_count, heads * head_dim), BF16),
            shape((row_count, heads * head_dim), F32),
            shape((row_count, head_dim), F32),
            shape((row_count, head_dim), F32),
            shape((2, row_count, head_dim), BF16),
        ),
        (info,),
        (q_all, g_all, p, merged, own_keys, own_values, low, ds, keys, values),
        (
            pltpu.VMEM((BLOCK, wide), BF16),
            pltpu.VMEM((BLOCK, wide), BF16),
        ),
        8 << 20,
    )
    going_out = (mine + got[0].astype(F32) + from_pair.astype(F32)).astype(BF16)
    going_out, own_away = lax.optimization_barrier((going_out, own_away))
    landed = across(going_out)
    got = to_core(own_away)
    from_pair = to_pair(summed(own_theirs, got))
    landed, got, from_pair = lax.optimization_barrier((landed, got, from_pair))
    back = across(call(scatter, "scatter", banded_shape, (info, picks), (landed,), scratch))
    grad_k, grad_v = call(
        unpack,
        "unpack",
        (shape((half_dim, row_count), F32),) * 2,
        (),
        (own_mine, got, from_pair, back),
    )
    return out, grad_queries, grad_k.T, grad_v.T


def solution(mesh):
    seq, heads = mesh.devices.shape
    split = Mesh(
        mesh.devices.reshape(seq // 2, 2, heads // 2, 2), ("z", "core", "grp", "pair")
    )
    spec = P(("z", "core"), ("grp", "pair"))
    return jax.shard_map(
        local,
        mesh=split,
        in_specs=(spec, spec, spec, P(), spec),
        out_specs=(spec, spec, spec, spec),
        check_vma=False,
    )
```

```python
import functools

import jax
import jax.numpy as jnp
from jax import lax
from jax.experimental import pallas as pl
from jax.experimental.pallas import tpu as pltpu
from jax.sharding import Mesh, PartitionSpec as P

BLOCK = 512
NEGATIVE = -1e30
NO_KEY = -1e4
SWAP = [(0, 1), (1, 0)]
LOG2_E = 1.4426950408889634
F32 = jnp.float32
BF16 = jnp.bfloat16
NT = (((1,), (1,)), ((), ()))
NN = (((1,), (0,)), ((), ()))
LIMIT = 4 << 20
STEP = 128


def first_rank(count):
    return count * 5 // 8


def offset_of(info, picks, block, slot):
    return picks[(block * info[4] + info[2]) * 2 + slot]


def rank_of_pick(info, picks, rank, slot, count):
    first = first_rank(count)
    block = (first + rank) % count
    picked = jnp.maximum(block - offset_of(info, picks, block, slot), 0)
    return jnp.where(picked >= first, picked - first, picked - first + count)


def dot(a, b, dims=NN):
    return lax.dot_general(a, b, dims, preferred_element_type=F32)


def first_half(shape):
    return lax.broadcasted_iota(jnp.int32, shape, len(shape) - 1) < shape[-1] // 2


def swap_halves(x):
    return pltpu.roll(x, x.shape[-1] // 2, x.ndim - 1)


def split_features(is_low, own, other):
    low = jnp.where(is_low, own, other)
    high = jnp.where(is_low, other, own)
    half = first_half(low.shape)
    return jnp.where(half, low, swap_halves(high)), jnp.where(half, swap_halves(low), high)


def join_features(is_low, k, v):
    half = first_half(k.shape)
    low = jnp.where(half, k, swap_halves(v))
    high = jnp.where(half, swap_halves(k), v)
    return jnp.where(is_low, low, high), jnp.where(is_low, high, low)


def load_tiles(pieces, is_low, key_scr, value_scr):
    rows = pieces[0][0].shape[0]
    for i, (own, other) in enumerate(pieces):
        k, v = split_features(is_low, own, other)
        at = slice(i * rows, (i + 1) * rows)
        key_scr[at, :] = k.astype(BF16)
        value_scr[at, :] = v.astype(BF16)


def spans_of(ref, rows):
    return [slice(at, at + rows) for at in range(0, ref.shape[0], rows)]


def own_scores(
    heads, info, q_all, g_all, own_a, own_b, own_c, own_d,
    p_ref, stats, key_scr, value_scr,
):
    rows, dim = q_all.shape[0] // heads, q_all.shape[1]
    rate = dim ** (-0.5) * LOG2_E
    pieces = [(own_a, own_b), (own_c, own_d)]
    pieces = [tuple(ref[...].astype(F32) for ref in piece) for piece in pieces]
    load_tiles(pieces, info[1] == 0, key_scr, value_scr)
    for h in range(heads):
        col = slice(h * rows, (h + 1) * rows)
        q, g = q_all[col, :], g_all[col, :]
        spans = spans_of(key_scr, rows)
        s = dot(key_scr[spans[0], :], q, NT)
        earlier = lax.broadcasted_iota(jnp.int32, s.shape, 0) <= lax.broadcasted_iota(
            jnp.int32, s.shape, 1
        )
        s = jnp.where(earlier, s, NEGATIVE)
        p_ref[spans[0], col] = s
        top = jnp.max(s, axis=0, keepdims=True)
        s = jnp.where(info[0] == 1, dot(key_scr[spans[1], :], q, NT), NEGATIVE)
        p_ref[spans[1], col] = s
        top = jnp.maximum(top, jnp.max(s, axis=0, keepdims=True))
        total = jnp.zeros_like(top)
        delta = jnp.zeros_like(top)
        for span in spans:
            p = jnp.exp2((p_ref[span, col] - top) * rate)
            dp = dot(value_scr[span, :], g, NT)
            p_ref[span, col] = p
            total = total + jnp.sum(p, axis=0, keepdims=True)
            delta = delta + jnp.sum(p * dp, axis=0, keepdims=True)
        stats[0:1, col] = top
        stats[1:2, col] = total
        stats[2:3, col] = delta


def picked_grads(
    heads, picked, info, picks, q_all, g_all, stats, x_ref, y_ref, xc_ref, yc_ref,
    mine_ref, theirs_ref, away_ref, low_ref, ds_ref, key_scr, value_scr, merged, s_scr, dp_scr,
):
    rows, dim = q_all.shape[0] // heads, q_all.shape[1]
    scaling = dim ** (-0.5)
    rate = scaling * LOG2_E
    is_low = info[1] == 0
    stripes = x_ref.shape[0]
    stripe = rows // stripes
    halves = [
        [ref[...].astype(F32).reshape(stripes, picked, stripe, dim) for ref in refs]
        for refs in ((x_ref, y_ref), (xc_ref, yc_ref))
    ]
    pieces = [
        tuple(part[:, j].reshape(rows, dim) for part in half) for j in range(picked) for half in halves
    ]
    load_tiles(pieces, is_low, key_scr, value_scr)
    spans = spans_of(key_scr, STEP)
    usable = [offset_of(info, picks, info[3], i * STEP // BLOCK) <= info[3] for i in range(len(spans))]
    for h in range(heads):
        col = slice(h * rows, (h + 1) * rows)
        q, g = q_all[col, :], g_all[col, :]
        own_top = stats[0:1, col]
        top = own_top
        for i, span in enumerate(spans):
            s = dot(key_scr[span, :], q, NT)
            s_scr[span, :] = s
            most = jnp.max(s, axis=0, keepdims=True)
            top = jnp.where(usable[i], jnp.maximum(top, most), top)
        shift = jnp.exp2((own_top - top) * rate)
        total = stats[1:2, col] * shift
        delta = stats[2:3, col] * shift
        for i, span in enumerate(spans):
            slope = jnp.where(usable[i], rate, 0.0)
            floor = jnp.where(usable[i], top * -rate, NO_KEY)
            p = jnp.exp2(s_scr[span, :] * slope + floor)
            dp = dot(value_scr[span, :], g, NT)
            s_scr[span, :] = p
            dp_scr[span, :] = dp
            total = total + jnp.sum(p, axis=0, keepdims=True)
            delta = delta + jnp.sum(p * dp, axis=0, keepdims=True)
        scale = 1.0 / total
        delta = delta * scale
        merged[0:1, col] = shift * scale
        merged[1:2, col] = delta
        for span in spans:
            p = s_scr[span, :] * scale
            low_ref[span, col] = p.astype(BF16)
            ds_ref[span, col] = (p * (dp_scr[span, :] - delta)).astype(BF16)
    parts = []
    for span in spans_of(key_scr, rows):
        k = dot(ds_ref[span, :], q_all[...]) * scaling
        v = dot(low_ref[span, :], g_all[...])
        parts.append(join_features(is_low, k, v))
    for half in range(2):
        a, b = (
            jnp.concatenate(
                [parts[2 * j + half][i].reshape(stripes, stripe, dim) for j in range(picked)], axis=1
            )
            for i in range(2)
        )
        if half == 0:
            mine_ref[...] = a
            theirs_ref[...] = b
        else:
            away_ref[0] = a.astype(BF16)
            away_ref[1] = b.astype(BF16)


def row_outputs(
    heads, info, q_all, g_all, p_ref, merged, own_keys, own_values, low_ref, ds_ref, keys, values,
    out_ref, dq_ref, own_mine, own_theirs, own_away, low_scr, ds_scr,
):
    rows, dim = q_all.shape[0] // heads, q_all.shape[1]
    scaling = dim ** (-0.5)
    spans = spans_of(p_ref, rows)
    own_kt, own_vt, key_t, value_t = (ref[...].T for ref in (own_keys, own_values, keys, values))
    for h in range(heads):
        lane = slice(h * dim, (h + 1) * dim)
        col = slice(h * rows, (h + 1) * rows)
        scale, delta = merged[0:1, col], merged[1:2, col]
        for span in spans:
            p = p_ref[span, col] * scale
            dp = dot(own_values[span, :], g_all[col, :], NT)
            low_scr[span, col] = p.astype(BF16)
            ds_scr[span, col] = (p * (dp - delta)).astype(BF16)
        out_t = dot(own_vt, low_scr[:, col]) + dot(value_t, low_ref[:, col])
        out_ref[:, lane] = out_t.T.astype(BF16)
        dq_t = dot(own_kt, ds_scr[:, col]) + dot(key_t, ds_ref[:, col])
        dq_ref[:, lane] = dq_t.T * scaling
    for i, span in enumerate(spans):
        k = dot(ds_scr[span, :], q_all[...]) * scaling
        v = dot(low_scr[span, :], g_all[...])
        a, b = join_features(info[1] == 0, k, v)
        if i == 0:
            own_mine[...] = a
            own_theirs[...] = b
        else:
            own_away[0] = a.astype(BF16)
            own_away[1] = b.astype(BF16)


def call(kernel, name, out_shape, scalars, arrays, scratch=(), limit=LIMIT, space=pltpu.VMEM):
    vmem = pl.BlockSpec(memory_space=pltpu.VMEM)
    smem = pl.BlockSpec(memory_space=pltpu.SMEM)
    return pl.pallas_call(
        kernel,
        out_shape=out_shape,
        in_specs=[smem] * len(scalars) + [pl.BlockSpec(memory_space=space)] * len(arrays),
        out_specs=jax.tree.map(lambda _: vmem, out_shape),
        scratch_shapes=list(scratch),
        compiler_params=pltpu.CompilerParams(vmem_limit_bytes=limit),
        name=name,
    )(*scalars, *arrays)


def pack(k_ref, v_ref, own_ref, striped_ref, k_scr, v_scr, sems):
    copies = [
        pltpu.make_async_copy(k_ref, k_scr, sems.at[0]),
        pltpu.make_async_copy(v_ref, v_scr, sems.at[1]),
    ]
    for copy in copies:
        copy.start()
    for copy in copies:
        copy.wait()
    both = jnp.concatenate([k_scr[...].astype(F32), v_scr[...].astype(F32)], 0).T
    own_ref[...] = both.astype(BF16)
    striped_ref[...] = both.reshape(striped_ref.shape).astype(BF16)


def stack_heads(q_ref, g_ref, q_all, g_all, sems):
    rows, dim = q_ref.shape[0], q_all.shape[1]
    heads = q_all.shape[0] // rows
    copies = [
        pltpu.make_async_copy(
            whole.at[:, pl.ds(h * dim, dim)],
            stacked.at[pl.ds(h * rows, rows), :],
            sems.at[i * heads + h],
        )
        for i, (whole, stacked) in enumerate(((q_ref, q_all), (g_ref, g_all)))
        for h in range(heads)
    ]
    for copy in copies:
        copy.start()
    for copy in copies:
        copy.wait()


def gather(info, picks, banded_ref, out_ref, scr):
    scr[...] = banded_ref[...].astype(F32)
    picked = out_ref.shape[1] // scr.shape[1]
    count = out_ref.shape[0]
    for rank in range(count):
        rows = [scr[rank_of_pick(info, picks, rank, j, count)] for j in range(picked)]
        out_ref[rank] = jnp.concatenate(rows, 0).astype(BF16)


def scatter(info, picks, landed_ref, out_ref, acc):
    acc[...] = jnp.zeros_like(acc)
    stripe = acc.shape[1]
    count = landed_ref.shape[0]
    for rank in range(count):
        rows = landed_ref[rank].astype(F32)
        for j in range(rows.shape[0] // stripe):
            at = rank_of_pick(info, picks, rank, j, count)
            acc[at] = acc[at] + rows[j * stripe : (j + 1) * stripe]
    out_ref[...] = acc[...].astype(BF16)


def unpack(mine_ref, got_ref, pair_ref, back_ref, gk_ref, gv_ref):
    total = mine_ref[...] + got_ref[0].astype(F32) + pair_ref[...].astype(F32)
    total = total + back_ref[...].astype(F32).reshape(total.shape)
    both = total.T
    gk_ref[...] = both[: gk_ref.shape[0]]
    gv_ref[...] = both[gk_ref.shape[0] :]


def local(queries, key_states, value_states, block_picks, grad_output):
    row_count = queries.shape[0]
    half_dim = key_states.shape[1]
    head_dim = 2 * half_dim
    z_count = lax.axis_size("z")
    picked = block_picks.shape[2]
    stripe = row_count // z_count
    axes = [lax.axis_index(name) for name in ("core", "pair", "grp", "z")]
    info = jnp.stack(axes + [jnp.int32(lax.axis_size("grp"))]).astype(jnp.int32)
    picks = block_picks.reshape(-1)
    shape = jax.ShapeDtypeStruct
    banded_shape = shape((z_count, stripe, head_dim), BF16)
    striped_shape = shape((z_count, picked * stripe, head_dim), BF16)

    def in_hbm(x):
        return pltpu.with_memory_space_constraint(x, pltpu.HBM)

    def to_pair(x):
        return lax.ppermute(x, "pair", SWAP)

    def to_core(x):
        return lax.ppermute(x, "core", SWAP)

    def across(x):
        order = [(first_rank(z_count) + i) % z_count for i in range(z_count)]
        return lax.all_to_all(
            x, "z", split_axis=0, concat_axis=0, axis_index_groups=[order], tiled=True
        )

    own, striped = call(
        pack,
        "pack",
        (shape((row_count, head_dim), BF16), banded_shape),
        (),
        tuple(in_hbm(x.T) for x in (key_states, value_states)),
        (
            pltpu.VMEM((half_dim, row_count), BF16),
            pltpu.VMEM((half_dim, row_count), BF16),
            pltpu.SemaphoreType.DMA((2,)),
        ),
        space=pltpu.HBM,
    )
    heads = queries.shape[1] // head_dim
    wide = heads * row_count
    many = picked * BLOCK
    banded = across(striped)
    own_pair = to_pair(own)
    banded, own, own_pair = lax.optimization_barrier((banded, own, own_pair))
    scratch = (pltpu.VMEM(banded_shape.shape, F32),)
    outgoing = call(gather, "gather", striped_shape, (info, picks), (banded,), scratch)
    outgoing, own, own_pair, queries, grad_output = lax.optimization_barrier(
        (outgoing, own, own_pair, queries, grad_output)
    )
    q_all, g_all = call(
        stack_heads,
        "stack_heads",
        (shape((wide, head_dim), BF16),) * 2,
        (),
        tuple(in_hbm(x) for x in (queries, grad_output)),
        (pltpu.SemaphoreType.DMA((2 * heads,)),),
        space=pltpu.HBM,
    )
    fetched = across(outgoing)
    own_block = call(
        functools.partial(own_scores, heads),
        "own_scores",
        (
            shape((BLOCK, wide), F32),
            shape((8, wide), F32),
            shape((BLOCK, head_dim), BF16),
            shape((BLOCK, head_dim), BF16),
        ),
        (info,),
        (q_all, g_all, own, own_pair, to_core(own), to_core(own_pair)),
        limit=6 << 20,
    )
    fetched, (p, stats, own_keys, own_values) = lax.optimization_barrier((fetched, own_block))
    fetched_pair = to_pair(fetched)
    fetched = (fetched, fetched_pair, to_core(fetched), to_core(fetched_pair))
    mine, theirs, away, low, ds, keys, values, merged = call(
        functools.partial(picked_grads, heads, picked),
        "picked_grads",
        (
            shape(striped_shape.shape, F32),
            shape(striped_shape.shape, F32),
            shape((2, *striped_shape.shape), BF16),
            shape((many, wide), BF16),
            shape((many, wide), BF16),
            shape((many, head_dim), BF16),
            shape((many, head_dim), BF16),
            shape((8, wide), F32),
        ),
        (info, picks),
        (q_all, g_all, stats, *fetched),
        (
            pltpu.VMEM((many, row_count), F32),
            pltpu.VMEM((many, row_count), F32),
        ),
        8 << 20,
    )

    def summed(theirs, got):
        return (theirs + got[1].astype(F32)).astype(BF16)

    got = to_core(away)
    from_pair = to_pair(summed(theirs, got))
    out, grad_queries, own_mine, own_theirs, own_away = call(
        functools.partial(row_outputs, heads),
        "row_outputs",
        (
            shape((row_count, heads * head_dim), BF16),
            shape((row_count, heads * head_dim), F32),
            shape((row_count, head_dim), F32),
            shape((row_count, head_dim), F32),
            shape((2, row_count, head_dim), BF16),
        ),
        (info,),
        (q_all, g_all, p, merged, own_keys, own_values, low, ds, keys, values),
        (
            pltpu.VMEM((BLOCK, wide), BF16),
            pltpu.VMEM((BLOCK, wide), BF16),
        ),
        8 << 20,
    )
    going_out = (mine + got[0].astype(F32) + from_pair.astype(F32)).astype(BF16)
    going_out, own_away = lax.optimization_barrier((going_out, own_away))
    landed = across(going_out)
    got = to_core(own_away)
    from_pair = to_pair(summed(own_theirs, got))
    landed, got, from_pair = lax.optimization_barrier((landed, got, from_pair))
    back = across(call(scatter, "scatter", banded_shape, (info, picks), (landed,), scratch))
    grad_k, grad_v = call(
        unpack,
        "unpack",
        (shape((half_dim, row_count), F32),) * 2,
        (),
        (own_mine, got, from_pair, back),
    )
    return out, grad_queries, grad_k.T, grad_v.T


def solution(mesh):
    seq, heads = mesh.devices.shape
    split = Mesh(
        mesh.devices.reshape(seq // 2, 2, heads // 2, 2), ("z", "core", "grp", "pair")
    )
    spec = P(("z", "core"), ("grp", "pair"))
    return jax.shard_map(
        local,
        mesh=split,
        in_specs=(spec, spec, spec, P(), spec),
        out_specs=(spec, spec, spec, spec),
        check_vma=False,
    )
```
